256 devices in a mesh: vocab: 32 (over y_hi, z, core), width: 8 (over x, y_lo).
Axes of the slice: x: 4, y: 4 (y_hi: 2, y_lo: 2; y = y_hi * 2 + y_lo), z: 8, core: 2. Of those that a mesh axis runs over, the one named last changes fastest.
Arguments:
- hidden: bfloat16 [256, 4608], P('vocab', 'width'), may hold values from -72 to 72
- pre_gain: float32 [4608], P('width'), may hold values from 0.1 to 1.9
- post_gain: float32 [4608], P('width'), may hold values from 0.1 to 1.9
- final_gain: float32 [4608], P('width'), may hold values from 0.1 to 1.9
- gate_weight: bfloat16 [4608, 18432], P('width', 'vocab'), may hold values from -0.09375 to 0.09375
- up_weight: bfloat16 [4608, 18432], P('width', 'vocab'), may hold values from -0.09375 to 0.09375
- down_weight: bfloat16 [18432, 4608], P('vocab', 'width'), may hold values from -2 to 2
- head_weight: bfloat16 [4608, 131072], P('width', 'vocab'), may hold values from -0.25 to 0.25
- token_ids: int32 [256], replicated, may hold values from 0 to 131071
- rewards: float32 [32], replicated, may hold values from -3 to 3
Outputs:
- grad_hidden: bfloat16 [256, 4608], P('vocab', 'width')
- grad_gate: bfloat16 [4608, 18432], P('width', 'vocab')
- grad_up: bfloat16 [4608, 18432], P('width', 'vocab')
- grad_down: bfloat16 [18432, 4608], P('vocab', 'width')
- grad_head: bfloat16 [4608, 131072], P('width', 'vocab')
- loss: float32 [], replicated
The draws below stay inside these ranges and needn't reach their ends.
All inputs are finite; a program needn't handle non-finite values.
Results may differ from the reference program's by a relative error of at most 0.013.
Values may be sent and summed in bfloat16 or wider, within the bound.
No kernel may reach another device: no remote copies, remote signals or barrier semaphores. Data moves between devices by JAX's collectives and lax.ppermute only.
A program may use at most 64 MiB of HBM per device.

```python
import math
import jax
import jax.numpy as jnp
from jax import lax

D = 4608
FF = 18432
VOCAB_DEV = 4096
LEN = 8
CAP = 30
TOKENS = 256
SEQS = 32
VOCAB = 131072


def draw_hidden(key, part):
    key_rows = jax.random.fold_in(key, 11)
    key_cols = jax.random.fold_in(key, 12)
    key_base = jax.random.fold_in(key, 13)
    row_scale = 0.3 * jnp.exp(jax.random.uniform(key_rows, (TOKENS, 1), jnp.float32, 0.0, math.log(10.0)))
    position = jnp.arange(D, dtype=jnp.float32)[None, :] / (D - 1)
    rough = jnp.exp(jax.random.uniform(key_cols, (1, D), jnp.float32, 0.0, math.log(4.0)))
    rising = jnp.exp(math.log(2.5) * position)
    base = jnp.clip(jax.random.normal(key_base, (TOKENS, D), jnp.float32), -6.0, 6.0)
    col_scale = 0.4 * rising * rough
    return (base * row_scale * col_scale).astype(jnp.bfloat16)


def draw_down_weight(key, part):
    key_base = jax.random.fold_in(key, 21)
    position = jnp.arange(D, dtype=jnp.float32)[None, :] / (D - 1) - 0.5
    rising = jnp.exp(math.log(2.5) * position)
    base = jnp.clip(jax.random.normal(key_base, (FF, D), jnp.float32), -6.0, 6.0)
    return (base * rising / math.sqrt(FF)).astype(jnp.bfloat16)


def with_ends(result, rng, smallest, high):
    longest = result.shape.index(max(result.shape))
    spots = []
    for shift in (0, 1):
        where = [jax.random.randint(jax.random.fold_in(rng, axis), (), 0, length) for axis, length in enumerate(result.shape)]
        where[longest] = (where[longest] + shift) % result.shape[longest]
        spots.append(tuple(where))
    return result.at[spots[0]].set(smallest).at[spots[1]].set(high)


def shard_levels(stream_key, shape, pieces, least, top_value):
    def one(axis_at, parts):
        steps = jax.random.uniform(jax.random.fold_in(jax.random.fold_in(stream_key, 6), axis_at), (parts,), jnp.float32, least / len(pieces), top_value / len(pieces))
        return jnp.repeat(jnp.exp(steps), shape[axis_at] // parts).reshape((-1,) + (1,) * (len(shape) - axis_at - 1))

    gain = one(*pieces[0])
    for cut in pieces[1:]:
        gain = gain * one(*cut)
    return gain


def normal_values(own_key, extent, width, limit, shards=(), kind=jnp.bfloat16):
    entries = width * jax.random.normal(own_key, extent, jnp.float32)
    if shards:
        entries = entries * shard_levels(own_key, extent, shards, -0.22, 0.18)
    return jnp.clip(entries, -limit, limit).astype(kind)


def setup_inputs(seed: int = 0) -> dict:
    key_list = jax.random.split(jax.random.key(seed), 11)
    hidden = draw_hidden(jax.random.fold_in(key_list[10], 71), 0)
    pre_gain = jnp.clip(1.0 + 0.18 * jax.random.normal(key_list[1], (D,), jnp.float32), 0.1, 1.9)
    post_gain = jnp.clip(1.0 + 0.18 * jax.random.normal(key_list[2], (D,), jnp.float32), 0.1, 1.9)
    final_gain = jnp.clip(1.0 + 0.18 * jax.random.normal(key_list[3], (D,), jnp.float32), 0.1, 1.9)
    gate_weight = normal_values(key_list[4], (D, FF), D ** -0.5, 0.09375, ((0, 8), (1, 32)))
    up_weight = normal_values(key_list[5], (D, FF), D ** -0.5, 0.09375, ((0, 8), (1, 32)))
    down_weight = draw_down_weight(jax.random.fold_in(key_list[10], 71), 0)
    head_weight = normal_values(key_list[7], (D, VOCAB), (D // 9) ** -0.5, 0.25, ((0, 8), (1, 32)))
    token_ids = with_ends(jax.random.randint(key_list[8], (TOKENS,), 0, VOCAB), jax.random.fold_in(key_list[8], 1), 0, VOCAB - 1).astype(jnp.int32)
    rewards = normal_values(key_list[9], (SEQS,), 1.0, 3.0, (), jnp.float32)
    return {"hidden": hidden, "pre_gain": pre_gain, "post_gain": post_gain, "final_gain": final_gain, "gate_weight": gate_weight, "up_weight": up_weight, "down_weight": down_weight, "head_weight": head_weight, "token_ids": token_ids, "rewards": rewards}


EPS = 1e-06
ROOT_TWO_PI = math.sqrt(2.0 / math.pi)

def gelu_value(value):
    inner = ROOT_TWO_PI * (value + 0.044715 * value * value * value)
    return 0.5 * value * (1.0 + jnp.tanh(inner))

def gelu_slope(value):
    bent = jnp.tanh(ROOT_TWO_PI * (value + 0.044715 * value * value * value))
    return 0.5 * (1.0 + bent) + 0.5 * value * (1.0 - bent * bent) * ROOT_TWO_PI * (1.0 + 3.0 * 0.044715 * value * value)

def reference(hidden, pre_gain, post_gain, final_gain, gate_weight, up_weight, down_weight, head_weight, token_ids, rewards):
    inputs = hidden.astype(jnp.float32)
    model = inputs.shape[1]
    scale_pre = lax.rsqrt(lax.optimization_barrier(jnp.sum(inputs * inputs, axis=1, keepdims=True)) / model + EPS)
    normed = (inputs * scale_pre * pre_gain).astype(jnp.bfloat16)
    gate = jnp.dot(normed, gate_weight, preferred_element_type=jnp.float32)
    upward = jnp.dot(normed, up_weight, preferred_element_type=jnp.float32)
    gelu_gate = gelu_value(gate)
    active = (gelu_gate * upward).astype(jnp.bfloat16)
    branch = jnp.dot(active, down_weight, preferred_element_type=jnp.float32)
    scale_post = lax.rsqrt(lax.optimization_barrier(jnp.sum(branch * branch, axis=1, keepdims=True)) / model + EPS)
    resid = inputs + branch * scale_post * post_gain
    scale_final = lax.rsqrt(lax.optimization_barrier(jnp.sum(resid * resid, axis=1, keepdims=True)) / model + EPS)
    final = (resid * scale_final * final_gain).astype(jnp.bfloat16)
    blocks_count = VOCAB // VOCAB_DEV
    blocks = jnp.moveaxis(head_weight.reshape(model, blocks_count, VOCAB_DEV), 1, 0)
    columns = jnp.arange(VOCAB, dtype=jnp.int32).reshape(blocks_count, VOCAB_DEV)

    def capped_block(block):
        logits = jnp.dot(final, block, preferred_element_type=jnp.float32)
        return CAP * jnp.tanh(logits / CAP)
    capped = lax.map(capped_block, blocks)
    hits = columns[:, None, :] == token_ids[None, :, None]
    total = lax.optimization_barrier(jnp.sum(jnp.exp(capped - CAP), axis=(0, 2)))
    target = lax.optimization_barrier(jnp.sum(jnp.where(hits, capped, 0.0), axis=(0, 2)))
    lognorm = CAP + jnp.log(total)
    logprob = target - lognorm
    weights = jnp.repeat(rewards, LEN)
    loss = -jnp.mean(weights * logprob)

    def second_pass(carry, item):
        block, capped_part, hit_part = item
        prob = jnp.exp(capped_part - lognorm[:, None])
        slope = 1.0 - (capped_part / CAP) ** 2
        delta = (-weights[:, None] * (hit_part.astype(jnp.float32) - prob) * slope).astype(jnp.bfloat16)
        grad_block = lax.dot_general(final, delta, (((0,), (0,)), ((), ())), preferred_element_type=jnp.float32).astype(jnp.bfloat16)
        carry = carry + lax.dot_general(delta, block, (((1,), (1,)), ((), ())), preferred_element_type=jnp.float32)
        return (carry, grad_block)
    grad_final, grad_blocks = lax.scan(second_pass, jnp.zeros(final.shape, jnp.float32), (blocks, capped, hits))
    grad_head = jnp.moveaxis(grad_blocks, 0, 1).reshape(model, VOCAB)
    weighted = grad_final * final_gain
    back_final = lax.optimization_barrier(jnp.sum(weighted * resid, axis=1, keepdims=True))
    grad_resid = scale_final * weighted - resid * scale_final ** 3 * back_final / model
    weighted_post = grad_resid * post_gain
    back_post = lax.optimization_barrier(jnp.sum(weighted_post * branch, axis=1, keepdims=True))
    grad_branch = (scale_post * weighted_post - branch * scale_post ** 3 * back_post / model).astype(jnp.bfloat16)
    grad_down = lax.dot_general(active, grad_branch, (((0,), (0,)), ((), ())), preferred_element_type=jnp.float32).astype(jnp.bfloat16)
    grad_active = lax.dot_general(grad_branch, down_weight, (((1,), (1,)), ((), ())), preferred_element_type=jnp.float32)
    grad_gate_in = (grad_active * upward * gelu_slope(gate)).astype(jnp.bfloat16)
    grad_up_in = (grad_active * gelu_gate).astype(jnp.bfloat16)
    grad_gate = lax.dot_general(normed, grad_gate_in, (((0,), (0,)), ((), ())), preferred_element_type=jnp.float32).astype(jnp.bfloat16)
    grad_up = lax.dot_general(normed, grad_up_in, (((0,), (0,)), ((), ())), preferred_element_type=jnp.float32).astype(jnp.bfloat16)
    grad_normed = lax.dot_general(grad_gate_in, gate_weight, (((1,), (1,)), ((), ())), preferred_element_type=jnp.float32)
    grad_normed = grad_normed + lax.dot_general(grad_up_in, up_weight, (((1,), (1,)), ((), ())), preferred_element_type=jnp.float32)
    weighted_pre = grad_normed * pre_gain
    back_pre = lax.optimization_barrier(jnp.sum(weighted_pre * inputs, axis=1, keepdims=True))
    grad_hidden = (grad_resid + scale_pre * weighted_pre - inputs * scale_pre ** 3 * back_pre / model).astype(jnp.bfloat16)
    return (grad_hidden, grad_gate, grad_up, grad_down, grad_head, loss)
```

```python
import math

import jax
import jax.numpy as jnp
from jax import lax
from jax.sharding import PartitionSpec as P

CAP = 30.0
EPS = 1e-06
ROOT_TWO_PI = math.sqrt(2.0 / math.pi)
BF16 = jnp.bfloat16
F32 = jnp.float32


def gelu_parts(value):
    square = value * value
    bent = jnp.tanh(ROOT_TWO_PI * value * (1.0 + 0.044715 * square))
    half = 0.5 * (1.0 + bent)
    slope = half + 0.5 * value * (1.0 - bent * bent) * ROOT_TWO_PI * (1.0 + 3.0 * 0.044715 * square)
    return value * half, slope


def contract(left, right, left_dim, right_dim):
    return lax.dot_general(
        left, right, (((left_dim,), (right_dim,)), ((), ())), preferred_element_type=F32
    )


def split(stat):
    high = lax.reduce_precision(stat, 8, 7)
    rest = stat - high
    low = lax.reduce_precision(rest, 8, 7)
    return [high.astype(BF16)[..., None], low.astype(BF16)[..., None]]


def joined(columns, at):
    return columns[..., at].astype(F32) + columns[..., at + 1].astype(F32)


def scatter_sum(parts, axis):
    size = lax.axis_size(axis)
    moved = lax.all_to_all(
        parts.reshape(size, parts.shape[0] // size, parts.shape[1]), axis, 0, 0, tiled=True
    )
    return jnp.sum(moved.astype(F32), axis=0)


def gather(piece, axis):
    size = lax.axis_size(axis)
    moved = lax.all_to_all(
        jnp.broadcast_to(piece[None], (size, *piece.shape)), axis, 0, 0, tiled=True
    )
    return moved.reshape(size * piece.shape[0], piece.shape[1])


def width_sums(stats):
    rows = jnp.stack(stats, axis=-1)
    size = lax.axis_size("width")
    moved = lax.all_to_all(
        jnp.broadcast_to(rows[None], (size, *rows.shape)), "width", 0, 0, tiled=True
    )
    return jnp.sum(moved, axis=0)


def shards(
    hidden,
    pre_gain,
    post_gain,
    final_gain,
    gate_weight,
    up_weight,
    down_weight,
    head_weight,
    token_ids,
    rewards,
):
    tok_dev, width_dev = hidden.shape
    tokens = token_ids.shape[0]
    model = width_dev * lax.axis_size("width")
    ff_dev = gate_weight.shape[1]
    vocab_dev = head_weight.shape[1]
    vocab_index = lax.axis_index("vocab")
    width_index = lax.axis_index("width")
    own_start = vocab_index * tok_dev
    sub_tok = tokens // lax.axis_size("width")
    sub_start = width_index * sub_tok

    weights = jnp.repeat(rewards, tokens // rewards.shape[0])
    own_weights = lax.dynamic_slice_in_dim(weights, own_start, tok_dev, 0)
    column_ids = vocab_index * vocab_dev + jnp.arange(vocab_dev, dtype=jnp.int32)
    hits = column_ids[None, :] == token_ids[:, None]
    sub_ids = lax.dynamic_slice_in_dim(token_ids, sub_start, sub_tok, 0)
    sub_hits = column_ids[None, :] == sub_ids[:, None]

    target_rows = scatter_sum(
        contract(hits.astype(BF16), head_weight, 1, 1).astype(BF16), "vocab"
    )

    inputs = gather(hidden, "vocab").astype(F32)
    scaled = (inputs * pre_gain).astype(BF16)
    gate_part = jnp.dot(scaled, gate_weight, preferred_element_type=F32)
    up_part = jnp.dot(scaled, up_weight, preferred_element_type=F32)
    squares_part = jnp.sum(inputs * inputs, axis=1)
    message = jnp.concatenate(
        [gate_part.astype(BF16), up_part.astype(BF16), *split(squares_part)], axis=1
    )
    sums = scatter_sum(message, "width")
    sub_squares = sums[:, 2 * ff_dev] + sums[:, 2 * ff_dev + 1]
    sub_scale = lax.rsqrt(sub_squares / model + EPS)[:, None]
    gate = sums[:, :ff_dev] * sub_scale
    upward = sums[:, ff_dev : 2 * ff_dev] * sub_scale
    gelu_gate, gelu_slope = gelu_parts(gate)
    sub_active = (gelu_gate * upward).astype(BF16)
    message = gather(jnp.concatenate([sub_active, *split(sub_squares)], axis=1), "width")
    active = message[:, :ff_dev]
    squares_pre = joined(message, ff_dev)
    scale_pre = lax.rsqrt(squares_pre / model + EPS)[:, None]
    normed = (inputs * scale_pre * pre_gain).astype(BF16)
    own_squares = lax.dynamic_slice_in_dim(squares_pre, own_start, tok_dev, 0)

    branch = scatter_sum(
        jnp.dot(active, down_weight, preferred_element_type=F32).astype(BF16), "vocab"
    )
    own_inputs = hidden.astype(F32)
    bent = branch * post_gain
    stats = width_sums(
        [
            jnp.sum(branch * branch, axis=1),
            jnp.sum(own_inputs * bent, axis=1),
            jnp.sum(bent * bent, axis=1),
        ]
    )
    scale_post = lax.rsqrt(stats[:, 0] / model + EPS)
    squares_final = own_squares + scale_post * (2.0 * stats[:, 1] + scale_post * stats[:, 2])
    scale_final = lax.rsqrt(jnp.maximum(squares_final, 0.0) / model + EPS)[:, None]
    scale_post = scale_post[:, None]
    resid = own_inputs + scale_post * bent
    final = gather((resid * scale_final * final_gain).astype(BF16), "vocab")

    logits = scatter_sum(
        jnp.dot(final, head_weight, preferred_element_type=F32).astype(BF16), "width"
    )
    capped = CAP * jnp.tanh(logits / CAP)
    slope = 1.0 - (capped / CAP) ** 2
    raised = jnp.where(sub_hits, 0.0, jnp.exp(capped - CAP))
    sloped = raised * slope
    others_part = jnp.sum(raised, axis=1)
    cross_part = jnp.sum(sloped * logits, axis=1)
    target_part = jnp.sum(jnp.where(sub_hits, logits, 0.0), axis=1)
    message = gather(
        jnp.concatenate(
            [
                sloped.astype(BF16),
                *split(others_part),
                *split(cross_part),
                *split(target_part),
            ],
            axis=1,
        ),
        "width",
    )
    sloped_all = message[:, :vocab_dev]
    rows_part = contract(sloped_all, head_weight, 1, 1)
    own_sums = scatter_sum(
        jnp.concatenate([rows_part.astype(BF16), message[:, vocab_dev:]], axis=1), "vocab"
    )
    others = own_sums[:, width_dev] + own_sums[:, width_dev + 1]
    cross = own_sums[:, width_dev + 2] + own_sums[:, width_dev + 3]
    target_logit = own_sums[:, width_dev + 4] + own_sums[:, width_dev + 5]
    target = CAP * jnp.tanh(target_logit / CAP)
    total = others + jnp.exp(target - CAP)
    logprob = target - (CAP + jnp.log(total))
    spread = own_weights / total
    pull = -spread * others * (1.0 - (target / CAP) ** 2)

    grad_final = spread[:, None] * own_sums[:, :width_dev] + pull[:, None] * target_rows
    back_final = (spread * cross + pull * target_logit)[:, None] / scale_final
    weighted = grad_final * final_gain
    grad_resid = scale_final * weighted - resid * scale_final**3 * back_final / model
    weighted_post = grad_resid * post_gain
    back_post = width_sums([jnp.sum(weighted_post * branch, axis=1)])
    grad_branch = scale_post * weighted_post - branch * scale_post**3 * back_post / model

    message = gather(
        jnp.concatenate(
            [
                grad_branch.astype(BF16),
                *split(spread),
                *split(pull),
                *split(own_weights * logprob),
            ],
            axis=1,
        ),
        "vocab",
    )
    grad_branch = message[:, :width_dev]
    spread_all = joined(message, width_dev)[:, None]
    pull_all = joined(message, width_dev + 2)[:, None]
    loss = -jnp.mean(joined(message, width_dev + 4))

    grad_active = scatter_sum(contract(grad_branch, down_weight, 1, 1).astype(BF16), "width")
    sub_gate_in = (grad_active * upward * gelu_slope).astype(BF16)
    sub_up_in = (grad_active * gelu_gate).astype(BF16)
    back_part = jnp.sum(
        sub_gate_in.astype(F32) * gate + sub_up_in.astype(F32) * upward, axis=1
    )
    message = gather(
        jnp.concatenate([sub_gate_in, sub_up_in, *split(back_part)], axis=1), "width"
    )
    grad_gate_in = message[:, :ff_dev]
    grad_up_in = message[:, ff_dev : 2 * ff_dev]
    normed_part = contract(grad_gate_in, gate_weight, 1, 1) + contract(grad_up_in, up_weight, 1, 1)
    own_sums = scatter_sum(
        jnp.concatenate([normed_part.astype(BF16), message[:, 2 * ff_dev :]], axis=1), "vocab"
    )

    delta = (spread_all * sloped_all.astype(F32) + jnp.where(hits, pull_all, 0.0)).astype(BF16)
    grad_head = contract(final, delta, 0, 0).astype(BF16)
    grad_down = contract(active, grad_branch, 0, 0).astype(BF16)
    grad_gate = contract(normed, grad_gate_in, 0, 0).astype(BF16)
    grad_up = contract(normed, grad_up_in, 0, 0).astype(BF16)

    own_scale = lax.rsqrt(own_squares / model + EPS)[:, None]
    back_pre = (own_sums[:, width_dev] + own_sums[:, width_dev + 1])[:, None] / own_scale
    weighted_pre = own_sums[:, :width_dev] * pre_gain
    grad_hidden = (
        grad_resid + own_scale * weighted_pre - own_inputs * own_scale**3 * back_pre / model
    ).astype(BF16)
    return (grad_hidden, grad_gate, grad_up, grad_down, grad_head, loss)


def solution(mesh):
    return jax.shard_map(
        shards,
        mesh=mesh,
        in_specs=(
            P("vocab", "width"),
            P("width"),
            P("width"),
            P("width"),
            P("width", "vocab"),
            P("width", "vocab"),
            P("vocab", "width"),
            P("width", "vocab"),
            P(),
            P(),
        ),
        out_specs=(
            P("vocab", "width"),
            P("width", "vocab"),
            P("width", "vocab"),
            P("vocab", "width"),
            P("width", "vocab"),
            P(),
        ),
        check_vma=False,
    )
```

```python
import math

import jax
import jax.numpy as jnp
from jax import lax
from jax.sharding import PartitionSpec as P

CAP = 30.0
EPS = 1e-06
ROOT_TWO_PI = math.sqrt(2.0 / math.pi)
BF16 = jnp.bfloat16
F32 = jnp.float32


def gelu_parts(value):
    square = value * value
    bent = jnp.tanh(ROOT_TWO_PI * value * (1.0 + 0.044715 * square))
    half = 0.5 * (1.0 + bent)
    slope = half + 0.5 * value * (1.0 - bent * bent) * ROOT_TWO_PI * (1.0 + 3.0 * 0.044715 * square)
    return value * half, slope


def contract(left, right, left_dim, right_dim):
    return lax.dot_general(
        left, right, (((left_dim,), (right_dim,)), ((), ())), preferred_element_type=F32
    )


def split(stat):
    high = lax.reduce_precision(stat, 8, 7)
    rest = stat - high
    low = lax.reduce_precision(rest, 8, 7)
    return [high.astype(BF16)[..., None], low.astype(BF16)[..., None]]


def joined(columns, at):
    return columns[..., at].astype(F32) + columns[..., at + 1].astype(F32)


def scatter_sum(parts, axis):
    size = lax.axis_size(axis)
    moved = lax.all_to_all(
        parts.reshape(size, parts.shape[0] // size, parts.shape[1]), axis, 0, 0, tiled=True
    )
    return jnp.sum(moved.astype(F32), axis=0)


def gather(piece, axis):
    size = lax.axis_size(axis)
    moved = lax.all_to_all(
        jnp.broadcast_to(piece[None], (size, *piece.shape)), axis, 0, 0, tiled=True
    )
    return moved.reshape(size * piece.shape[0], piece.shape[1])


def shards(
    hidden,
    pre_gain,
    post_gain,
    final_gain,
    gate_weight,
    up_weight,
    down_weight,
    head_weight,
    token_ids,
    rewards,
):
    tok_dev, width_dev = hidden.shape
    tokens = token_ids.shape[0]
    model = width_dev * lax.axis_size("width")
    ff_dev = gate_weight.shape[1]
    vocab_dev = head_weight.shape[1]
    vocab_index = lax.axis_index("vocab")
    width_index = lax.axis_index("width")
    own_start = vocab_index * tok_dev
    sub_tok = tokens // lax.axis_size("width")
    sub_start = width_index * sub_tok

    weights = jnp.repeat(rewards, tokens // rewards.shape[0])
    own_weights = lax.dynamic_slice_in_dim(weights, own_start, tok_dev, 0)
    column_ids = vocab_index * vocab_dev + jnp.arange(vocab_dev, dtype=jnp.int32)
    hits = column_ids[None, :] == token_ids[:, None]
    sub_ids = lax.dynamic_slice_in_dim(token_ids, sub_start, sub_tok, 0)
    sub_hits = column_ids[None, :] == sub_ids[:, None]

    target_part = contract(hits.astype(BF16), head_weight, 1, 1).astype(BF16)

    inputs = gather(hidden, "vocab").astype(F32)
    first_logits = lax.psum_scatter(
        jnp.dot((inputs * final_gain).astype(BF16), head_weight, preferred_element_type=F32),
        "width",
        scatter_dimension=0,
        tiled=True,
    )
    scaled = (inputs * pre_gain).astype(BF16)
    gate_part = jnp.dot(scaled, gate_weight, preferred_element_type=F32)
    up_part = jnp.dot(scaled, up_weight, preferred_element_type=F32)
    squares_part = jnp.sum(inputs * inputs, axis=1)
    message = jnp.concatenate(
        [gate_part.astype(BF16), up_part.astype(BF16), *split(squares_part)], axis=1
    )
    sums = scatter_sum(message, "width")
    sub_squares = sums[:, 2 * ff_dev] + sums[:, 2 * ff_dev + 1]
    sub_scale = lax.rsqrt(sub_squares / model + EPS)[:, None]
    gate = sums[:, :ff_dev] * sub_scale
    upward = sums[:, ff_dev : 2 * ff_dev] * sub_scale
    gelu_gate, gelu_slope = gelu_parts(gate)
    sub_active = (gelu_gate * upward).astype(BF16)
    message = gather(jnp.concatenate([sub_active, *split(sub_squares)], axis=1), "width")
    active = message[:, :ff_dev]
    squares_pre = joined(message, ff_dev)
    scale_pre = lax.rsqrt(squares_pre / model + EPS)[:, None]
    normed = (inputs * scale_pre * pre_gain).astype(BF16)
    own_squares = lax.dynamic_slice_in_dim(squares_pre, own_start, tok_dev, 0)

    own_sums = scatter_sum(
        jnp.concatenate(
            [jnp.dot(active, down_weight, preferred_element_type=F32).astype(BF16), target_part],
            axis=1,
        ),
        "vocab",
    )
    branch = own_sums[:, :width_dev]
    target_rows = own_sums[:, width_dev:]
    own_inputs = hidden.astype(F32)
    bent = branch * post_gain
    message = gather(
        jnp.concatenate(
            [
                branch.astype(BF16),
                *split(jnp.sum(branch * branch, axis=1)),
                *split(jnp.sum(own_inputs * bent, axis=1)),
                *split(jnp.sum(bent * bent, axis=1)),
            ],
            axis=1,
        ),
        "vocab",
    )
    branch_all = message[:, :width_dev].astype(F32)
    second_part = jnp.dot(
        (branch_all * (post_gain * final_gain)).astype(BF16),
        head_weight,
        preferred_element_type=F32,
    ).astype(BF16)
    sums = scatter_sum(jnp.concatenate([second_part, message[:, width_dev:]], axis=1), "width")
    second_logits = sums[:, :vocab_dev]
    stats = [sums[:, vocab_dev + 2 * i] + sums[:, vocab_dev + 2 * i + 1] for i in range(3)]
    sub_post = lax.rsqrt(stats[0] / model + EPS)
    along = stats[1] + sub_post * stats[2]
    squares_final = sub_squares + sub_post * (stats[1] + along)
    sub_final = lax.rsqrt(jnp.maximum(squares_final, 0.0) / model + EPS)
    logits = sub_final[:, None] * (first_logits + sub_post[:, None] * second_logits)
    capped = CAP * jnp.tanh(logits / CAP)
    slope = 1.0 - (capped / CAP) ** 2
    raised = jnp.where(sub_hits, 0.0, jnp.exp(capped - CAP))
    sloped = raised * slope
    stats = [
        jnp.sum(raised, axis=1),
        jnp.sum(sloped * logits, axis=1),
        jnp.sum(sloped * second_logits, axis=1),
        jnp.sum(jnp.where(sub_hits, logits, 0.0), axis=1),
        jnp.sum(jnp.where(sub_hits, second_logits, 0.0), axis=1),
    ]
    columns = [c for stat in [*stats, sub_post, sub_final, along] for c in split(stat)]
    message = gather(jnp.concatenate([sloped.astype(BF16), *columns], axis=1), "width")
    sloped_all = message[:, :vocab_dev]
    rows_part = contract(sloped_all, head_weight, 1, 1)
    stats_all = message[:, vocab_dev:]
    post_all = joined(stats_all, 10)[:, None]
    final_all = joined(stats_all, 12)[:, None]
    own_stats = lax.dynamic_slice_in_dim(stats_all, own_start, tok_dev, 0)
    scale_post = joined(own_stats, 10)[:, None]
    scale_final = joined(own_stats, 12)[:, None]
    along = joined(own_stats, 14)[:, None]
    own_sums = scatter_sum(
        jnp.concatenate([rows_part.astype(BF16), stats_all[:, :10]], axis=1), "vocab"
    )
    others, cross, cross_second, target_logit, target_second = [
        own_sums[:, width_dev + 2 * i] + own_sums[:, width_dev + 2 * i + 1] for i in range(5)
    ]
    target = CAP * jnp.tanh(target_logit / CAP)
    total = others + jnp.exp(target - CAP)
    logprob = target - (CAP + jnp.log(total))
    spread = own_weights / total
    pull = -spread * others * (1.0 - (target / CAP) ** 2)

    grad_final = spread[:, None] * own_sums[:, :width_dev] + pull[:, None] * target_rows
    back_final = (spread * cross + pull * target_logit)[:, None] / scale_final
    resid = own_inputs + scale_post * bent
    weighted = grad_final * final_gain
    grad_resid = scale_final * weighted - resid * scale_final**3 * back_final / model
    weighted_post = grad_resid * post_gain
    back_post = (
        scale_final * (spread * cross_second + pull * target_second)[:, None]
        - scale_final**3 * back_final / model * along
    )
    grad_branch = scale_post * weighted_post - branch * scale_post**3 * back_post / model

    message = gather(
        jnp.concatenate(
            [
                grad_branch.astype(BF16),
                *split(spread),
                *split(pull),
                *split(own_weights * logprob),
            ],
            axis=1,
        ),
        "vocab",
    )
    grad_branch = message[:, :width_dev]
    spread_all = joined(message, width_dev)[:, None]
    pull_all = joined(message, width_dev + 2)[:, None]
    loss = -jnp.mean(joined(message, width_dev + 4))

    grad_active = scatter_sum(contract(grad_branch, down_weight, 1, 1).astype(BF16), "width")
    sub_gate_in = (grad_active * upward * gelu_slope).astype(BF16)
    sub_up_in = (grad_active * gelu_gate).astype(BF16)
    back_part = jnp.sum(
        sub_gate_in.astype(F32) * gate + sub_up_in.astype(F32) * upward, axis=1
    )
    message = gather(
        jnp.concatenate([sub_gate_in, sub_up_in, *split(back_part)], axis=1), "width"
    )
    grad_gate_in = message[:, :ff_dev]
    grad_up_in = message[:, ff_dev : 2 * ff_dev]
    normed_part = contract(grad_gate_in, gate_weight, 1, 1) + contract(grad_up_in, up_weight, 1, 1)
    own_sums = scatter_sum(
        jnp.concatenate([normed_part.astype(BF16), message[:, 2 * ff_dev :]], axis=1), "vocab"
    )

    delta = (spread_all * sloped_all.astype(F32) + jnp.where(hits, pull_all, 0.0)).astype(BF16)
    final = ((inputs + post_all * branch_all * post_gain) * final_all * final_gain).astype(BF16)
    grad_head = contract(final, delta, 0, 0).astype(BF16)
    grad_down = contract(active, grad_branch, 0, 0).astype(BF16)
    grad_gate = contract(normed, grad_gate_in, 0, 0).astype(BF16)
    grad_up = contract(normed, grad_up_in, 0, 0).astype(BF16)

    own_scale = lax.rsqrt(own_squares / model + EPS)[:, None]
    back_pre = (own_sums[:, width_dev] + own_sums[:, width_dev + 1])[:, None] / own_scale
    weighted_pre = own_sums[:, :width_dev] * pre_gain
    grad_hidden = (
        grad_resid + own_scale * weighted_pre - own_inputs * own_scale**3 * back_pre / model
    ).astype(BF16)
    return (grad_hidden, grad_gate, grad_up, grad_down, grad_head, loss)


def solution(mesh):
    return jax.shard_map(
        shards,
        mesh=mesh,
        in_specs=(
            P("vocab", "width"),
            P("width"),
            P("width"),
            P("width"),
            P("width", "vocab"),
            P("width", "vocab"),
            P("vocab", "width"),
            P("width", "vocab"),
            P(),
            P(),
        ),
        out_specs=(
            P("vocab", "width"),
            P("width", "vocab"),
            P("width", "vocab"),
            P("vocab", "width"),
            P("width", "vocab"),
            P(),
        ),
        check_vma=False,
    )
```

```python
import math

import jax
import jax.numpy as jnp
from jax import lax
from jax.experimental import pallas as pl
from jax.experimental.pallas import tpu as pltpu
from jax.sharding import PartitionSpec as P

CAP = 30.0
EPS = 1e-06
ROOT_TWO_PI = math.sqrt(2.0 / math.pi)
BF16 = jnp.bfloat16
F32 = jnp.float32
LANES = 128
CHUNK = 512


def contract(left, right, left_dim, right_dim):
    return lax.dot_general(
        left, right, (((left_dim,), (right_dim,)), ((), ())), preferred_element_type=F32
    )


def gelu_parts(value):
    square = value * value
    bent = jnp.tanh(ROOT_TWO_PI * value * (1.0 + 0.044715 * square))
    half = 0.5 * (1.0 + bent)
    slope = half + 0.5 * value * (1.0 - bent * bent) * ROOT_TWO_PI * (1.0 + 3.0 * 0.044715 * square)
    return value * half, slope


def padded(width):
    return width // LANES * LANES + LANES


def pick(tile, at):
    lane = lax.broadcasted_iota(jnp.int32, tile.shape, 1)
    return jnp.sum(jnp.where((lane == at) | (lane == at + 1), tile, 0.0), axis=1, keepdims=True)


def read_stats(tile, width, count):
    return [pick(tile, width % LANES + 2 * i) for i in range(count)]


def tail_of(width):
    return slice(width // LANES * LANES, padded(width))


def with_stats(tile, width, stats):
    lane = lax.broadcasted_iota(jnp.int32, tile.shape, 1)
    at = width % LANES
    tile = jnp.where(lane < at, tile, 0.0)
    for i, stat in enumerate(stats):
        high = stat.astype(BF16).astype(F32)
        tile = jnp.where(lane == at + 2 * i, high, tile)
        tile = jnp.where(lane == at + 2 * i + 1, stat - high, tile)
    return tile.astype(BF16)


def put(ref, block, stats):
    width = block.shape[1]
    ref[:, :width] = block
    tail = tail_of(width)
    ref[:, tail] = with_stats(ref[:, tail].astype(F32), width, stats)


def put_copies(ref, block, stats):
    put(ref.at[0], block, stats)
    whole = ref[0]
    for i in range(1, ref.shape[0]):
        ref[i] = whole


def summed(ref, columns):
    total = ref[0, :, columns].astype(F32)
    for i in range(1, ref.shape[0]):
        total = total + ref[i, :, columns].astype(F32)
    return total


def local(body, outs, *args, scratch=(), hbm=(), smem=()):
    spaces = {**{i: pl.ANY for i in hbm}, **{i: pltpu.SMEM for i in smem}}
    return pl.pallas_call(
        body,
        out_shape=tuple(jax.ShapeDtypeStruct(s, d) for s, d in outs),
        in_specs=[
            pl.BlockSpec(memory_space=spaces.get(i, pltpu.VMEM)) for i in range(len(args))
        ],
        out_specs=tuple(pl.BlockSpec(memory_space=pltpu.VMEM) for _ in outs),
        scratch_shapes=scratch,
        compiler_params=pltpu.CompilerParams(vmem_limit_bytes=40 << 20),
    )(*args)


def exchange(parts, axis):
    size = lax.axis_size(axis)
    if parts.ndim == 2:
        parts = parts.reshape(size, parts.shape[0] // size, parts.shape[1])
    return lax.all_to_all(parts, axis, 0, 0, tiled=True)


def flat(message):
    return message.reshape(message.shape[0] * message.shape[1], message.shape[2])


def chunk_copies(source, buffer, sems):
    width = buffer.shape[2]
    return [
        pltpu.make_async_copy(source.at[:, pl.ds(i * width, width)], buffer.at[i], sems.at[i])
        for i in range(buffer.shape[0])
    ]


def gate_step(inputs, pre_gain, gate_weight, up_weight, out):
    width = gate_weight.shape[1]
    values = inputs[...].astype(F32)
    scaled = (values * pre_gain[...]).astype(BF16)
    squares = jnp.sum(values * values, axis=1, keepdims=True)
    put(out, contract(scaled, gate_weight[...], 1, 0).astype(BF16), [squares])
    out[:, padded(width) : padded(width) + width] = contract(
        scaled, up_weight[...], 1, 0
    ).astype(BF16)


def active_step(model, width, message, gate, upward, gelu_gate, gelu_slope, out):
    (squares,) = read_stats(summed(message, tail_of(width)), width, 1)
    scale = lax.rsqrt(squares / model + EPS)
    gate_value = summed(message, slice(0, width)) * scale
    up_value = summed(message, slice(padded(width), padded(width) + width)) * scale
    value, slope = gelu_parts(gate_value)
    gate[...] = gate_value
    upward[...] = up_value
    gelu_gate[...] = value
    gelu_slope[...] = slope
    put_copies(out, (value * up_value).astype(BF16), [squares])


def branch_step(message, down_weight, target_rows, out):
    width = down_weight.shape[0]
    depth = down_weight.shape[1]
    out[:, :depth] = contract(message[:, :width], down_weight[...], 1, 0).astype(BF16)
    out[:, padded(depth) : padded(depth) + depth] = target_rows[...]


def norm_step(message, inputs, post_gain, branch, target, out):
    width = branch.shape[1]
    value = summed(message, slice(0, width))
    branch[...] = value
    target[...] = summed(message, slice(padded(width), padded(width) + width))
    bent = value * post_gain[...]
    stats = [
        jnp.sum(value * value, axis=1, keepdims=True),
        jnp.sum(inputs[...].astype(F32) * bent, axis=1, keepdims=True),
        jnp.sum(bent * bent, axis=1, keepdims=True),
    ]
    lane = lax.broadcasted_iota(jnp.int32, out.shape[1:], 1)
    tile = jnp.zeros(out.shape[1:], F32)
    for i, stat in enumerate(stats):
        tile = jnp.where(lane == i, stat, tile)
    for i in range(out.shape[0]):
        out[i] = tile


def scale_step(model, ff_width, index, message, active, branch, scale_post, scale_final, out):
    tile = message[0]
    for i in range(1, message.shape[0]):
        tile = tile + message[i]
    lane = lax.broadcasted_iota(jnp.int32, tile.shape, 1)
    square, cross, bent = [
        jnp.sum(jnp.where(lane == i, tile, 0.0), axis=1, keepdims=True) for i in range(3)
    ]
    rows = pl.ds(pl.multiple_of(index[0] * tile.shape[0], tile.shape[0]), tile.shape[0])
    (own_squares,) = read_stats(active[rows, tail_of(ff_width)].astype(F32), ff_width, 1)
    post = lax.rsqrt(square / model + EPS)
    final_squares = own_squares + post * (2.0 * cross + post * bent)
    final = lax.rsqrt(jnp.maximum(final_squares, 0.0) / model + EPS)
    scale_post[...] = post
    scale_final[...] = final
    put_copies(out, branch[...].astype(BF16), [post, final])


def logit_step(message, inputs, post_gain, final_gain, down_weight, head, out, final, buffer, sems):
    copies = chunk_copies(head, buffer, sems)
    for copy in copies:
        copy.start()
    width = final.shape[1]
    branch = message[:, :width]
    post, scale = read_stats(message[:, tail_of(width)].astype(F32), width, 2)
    resid = inputs[...].astype(F32) + branch.astype(F32) * post * post_gain[...]
    final[...] = (resid * scale * final_gain[...]).astype(BF16)
    chunk = buffer.shape[2]
    vocab = chunk * buffer.shape[0]
    out[:, vocab : vocab + down_weight.shape[0]] = contract(
        branch, down_weight[...], 1, 1
    ).astype(BF16)
    for i, copy in enumerate(copies):
        copy.wait()
        out[:, i * chunk : (i + 1) * chunk] = contract(final[...], buffer[i], 1, 0).astype(BF16)


def soft_step(vocab, message, ids, out, branch_down):
    rows = message.shape[1]
    step = 256
    others = jnp.zeros((rows, step), F32)
    cross = jnp.zeros((rows, step), F32)
    target = jnp.zeros((rows, step), F32)
    lane = lax.broadcasted_iota(jnp.int32, (rows, step), 1)
    for i in range(vocab // step):
        columns = slice(i * step, (i + 1) * step)
        logits = summed(message, columns)
        hits = lane == ids[...] - i * step
        bent = jnp.tanh(logits / CAP)
        raised = jnp.where(hits, 0.0, jnp.exp(CAP * bent - CAP))
        sloped = raised * (1.0 - bent * bent)
        others = others + raised
        cross = cross + sloped * logits
        target = target + jnp.where(hits, logits, 0.0)
        part = sloped.astype(BF16)
        for j in range(out.shape[0]):
            out[j, :, columns] = part
    stats = [jnp.sum(x, axis=1, keepdims=True) for x in (others, cross, target)]
    tile = with_stats(jnp.zeros((rows, LANES), F32), vocab, stats)
    for j in range(out.shape[0]):
        out[j, :, vocab : vocab + LANES] = tile
    branch_down[...] = summed(message, slice(vocab, vocab + branch_down.shape[1]))


def row_step(message, head, out, buffer, sems):
    copies = chunk_copies(head, buffer, sems)
    for copy in copies:
        copy.start()
    chunk = buffer.shape[2]
    vocab = chunk * buffer.shape[0]
    total = jnp.zeros((message.shape[0], buffer.shape[1]), F32)
    for i, copy in enumerate(copies):
        copy.wait()
        total = total + contract(message[:, i * chunk : (i + 1) * chunk], buffer[i], 1, 1)
    put(
        out,
        total.astype(BF16),
        read_stats(message[:, vocab : vocab + LANES].astype(F32), vocab, 3),
    )


def resid_step(
    model,
    message,
    target_rows,
    branch,
    inputs,
    scale_post,
    scale_final,
    weights,
    post_gain,
    final_gain,
    grad_resid,
    out,
):
    width = branch.shape[1]
    others, cross, logit = read_stats(summed(message, tail_of(width)), width, 3)
    bent = jnp.tanh(logit / CAP)
    target = CAP * bent
    total = others + jnp.exp(target - CAP)
    logprob = target - CAP - jnp.log(total)
    spread = weights[...] / total
    pull = -spread * others * (1.0 - bent * bent)
    post = scale_post[...]
    final = scale_final[...]
    grad_final = spread * summed(message, slice(0, width)) + pull * target_rows[...]
    back_final = (spread * cross + pull * logit) / final
    value = branch[...]
    resid = inputs[...].astype(F32) + post * value * post_gain[...]
    grad = final * grad_final * final_gain[...] - resid * (
        final * final * final * back_final / model
    )
    grad_resid[...] = grad
    weighted = grad * post_gain[...]
    back_post = jnp.sum(weighted * value, axis=1, keepdims=True)
    put_copies(
        out,
        (post * weighted).astype(BF16),
        [spread, pull, weights[...] * logprob, back_post],
    )


def down_step(message, down_weight, out, loss):
    width = down_weight.shape[1]
    _, _, score, back_post = read_stats(message[:, tail_of(width)].astype(F32), width, 4)
    put(
        out,
        contract(message[:, :width], down_weight[...], 1, 1).astype(BF16),
        [back_post],
    )
    loss[...] = -jnp.sum(score, axis=0, keepdims=True) / message.shape[0]


def hidden_step(
    model, depth, index, message, branch_down, gate, upward, gelu_gate, gelu_slope, scales, out
):
    rows, width = gate.shape
    (back_post,) = read_stats(summed(message, tail_of(width)), width, 1)
    own = pl.ds(pl.multiple_of(index[0] * rows, rows), rows)
    (post,) = read_stats(scales[own, tail_of(depth)].astype(F32), depth, 1)
    grad = summed(message, slice(0, width)) - branch_down[...] * (
        post * post * post * back_post / model
    )
    gate_in = (grad * upward[...] * gelu_slope[...]).astype(BF16)
    up_in = (grad * gelu_gate[...]).astype(BF16)
    back = jnp.sum(
        gate_in.astype(F32) * gate[...] + up_in.astype(F32) * upward[...], axis=1, keepdims=True
    )
    start = padded(width)
    put(out.at[0], gate_in, [back, back_post])
    out[0, :, start : start + width] = up_in
    whole = out[0]
    for i in range(1, out.shape[0]):
        out[i] = whole


def normed_step(message, gate_weight, up_weight, out):
    width = gate_weight.shape[1]
    start = padded(width)
    total = contract(message[:, :width], gate_weight[...], 1, 1) + contract(
        message[:, start : start + width], up_weight[...], 1, 1
    )
    put(
        out,
        total.astype(BF16),
        read_stats(message[:, tail_of(width)].astype(F32), width, 1),
    )


def last_step(model, ff_width, index, message, grad_resid, inputs, active, pre_gain, out):
    rows, width = out.shape
    own = pl.ds(pl.multiple_of(index[0] * rows, rows), rows)
    (squares,) = read_stats(active[own, tail_of(ff_width)].astype(F32), ff_width, 1)
    scale = lax.rsqrt(squares / model + EPS)
    (back,) = read_stats(summed(message, tail_of(width)), width, 1)
    weighted = summed(message, slice(0, width)) * pre_gain[...]
    out[...] = (
        grad_resid[...] + scale * weighted - inputs[...].astype(F32) * (scale * scale * back / model)
    ).astype(BF16)


def joined(message, width, i):
    at = width + 2 * i
    return message[:, at : at + 1].astype(F32) + message[:, at + 1 : at + 2].astype(F32)


def shards(
    hidden,
    pre_gain,
    post_gain,
    final_gain,
    gate_weight,
    up_weight,
    down_weight,
    head_weight,
    token_ids,
    rewards,
):
    tok_dev, width = hidden.shape
    tokens = token_ids.shape[0]
    rows_n = lax.axis_size("vocab")
    cols_n = lax.axis_size("width")
    model = width * cols_n
    ff = gate_weight.shape[1]
    vocab = head_weight.shape[1]
    sub = tokens // cols_n
    vocab_index = lax.axis_index("vocab")
    width_index = lax.axis_index("width")
    row_at = vocab_index[None].astype(jnp.int32)
    col_at = width_index[None].astype(jnp.int32)
    pre_gain = pre_gain[None, :]
    post_gain = post_gain[None, :]
    final_gain = final_gain[None, :]

    weights = jnp.repeat(rewards, tokens // rewards.shape[0])
    own_weights = lax.dynamic_slice_in_dim(weights, vocab_index * tok_dev, tok_dev, 0)[:, None]
    ids = token_ids - vocab_index * vocab
    hits = jnp.arange(vocab, dtype=jnp.int32)[None, :] == ids[:, None]
    sub_ids = lax.dynamic_slice_in_dim(ids, width_index * sub, sub, 0)[:, None]
    target_part = contract(hits.astype(BF16), head_weight, 1, 1).astype(BF16)
    buffer = (
        pltpu.VMEM((vocab // CHUNK, width, CHUNK), BF16),
        pltpu.SemaphoreType.DMA((vocab // CHUNK,)),
    )

    inputs = flat(exchange(jnp.broadcast_to(hidden[None], (rows_n, tok_dev, width)), "vocab"))
    (message,) = local(
        gate_step,
        [((tokens, padded(ff) * 2), BF16)],
        inputs,
        pre_gain,
        gate_weight,
        up_weight,
    )
    gate, upward, gelu_gate, gelu_slope, message = local(
        lambda *refs: active_step(model, ff, *refs),
        [((sub, ff), F32)] * 4 + [((cols_n, sub, padded(ff)), BF16)],
        exchange(message, "width"),
    )
    active = flat(exchange(message, "width"))
    (message,) = local(
        branch_step, [((tokens, padded(width) * 2), BF16)], active, down_weight, target_part
    )
    branch, target_rows, message = local(
        norm_step,
        [((tok_dev, width), F32)] * 2 + [((cols_n, tok_dev, LANES), F32)],
        exchange(message, "vocab"),
        hidden,
        post_gain,
    )
    scale_post, scale_final, message = local(
        lambda *refs: scale_step(model, ff, *refs),
        [((tok_dev, 1), F32)] * 2 + [((rows_n, tok_dev, padded(width)), BF16)],
        row_at,
        exchange(message, "width"),
        active,
        branch,
        smem=(0,),
    )
    branch_all = flat(exchange(message, "vocab"))
    message, final = local(
        logit_step,
        [((tokens, vocab + ff), BF16), ((tokens, width), BF16)],
        branch_all,
        inputs,
        post_gain,
        final_gain,
        down_weight,
        head_weight,
        scratch=buffer,
        hbm=(5,),
    )
    message, branch_down = local(
        lambda *refs: soft_step(vocab, *refs),
        [((cols_n, sub, vocab + LANES), BF16), ((sub, ff), F32)],
        exchange(message, "width"),
        sub_ids,
    )
    sloped = flat(exchange(message, "width"))
    (message,) = local(
        row_step,
        [((tokens, padded(width)), BF16)],
        sloped,
        head_weight,
        scratch=buffer,
        hbm=(1,),
    )
    grad_resid, message = local(
        lambda *refs: resid_step(model, *refs),
        [((tok_dev, width), F32), ((rows_n, tok_dev, padded(width)), BF16)],
        exchange(message, "vocab"),
        target_rows,
        branch,
        hidden,
        scale_post,
        scale_final,
        own_weights,
        post_gain,
        final_gain,
    )
    weighted = flat(exchange(message, "vocab"))
    message, loss = local(
        down_step,
        [((tokens, padded(ff)), BF16), ((1, 1), F32)],
        weighted,
        down_weight,
    )
    (message,) = local(
        lambda *refs: hidden_step(model, width, *refs),
        [((cols_n, sub, padded(ff) * 2), BF16)],
        col_at,
        exchange(message, "width"),
        branch_down,
        gate,
        upward,
        gelu_gate,
        gelu_slope,
        branch_all,
        smem=(0,),
    )
    grads_in = flat(exchange(message, "width"))
    (message,) = local(
        normed_step, [((tokens, padded(width)), BF16)], grads_in, gate_weight, up_weight
    )
    (grad_hidden,) = local(
        lambda *refs: last_step(model, ff, *refs),
        [((tok_dev, width), BF16)],
        row_at,
        exchange(message, "vocab"),
        grad_resid,
        hidden,
        active,
        pre_gain,
        smem=(0,),
    )

    spread = joined(weighted, width, 0)
    pull = joined(weighted, width, 1)
    delta = (spread * sloped[:, :vocab].astype(F32) + jnp.where(hits, pull, 0.0)).astype(BF16)
    grad_head = contract(final, delta, 0, 0).astype(BF16)
    post = joined(branch_all, width, 0)
    back_post = joined(grads_in, ff, 1)
    grad_branch = (
        weighted[:, :width].astype(F32)
        - branch_all[:, :width].astype(F32) * (post**3 * back_post / model)
    ).astype(BF16)
    grad_down = contract(active[:, :ff], grad_branch, 0, 0).astype(BF16)
    scale_pre = lax.rsqrt(joined(active, ff, 0) / model + EPS)
    normed = (inputs.astype(F32) * scale_pre * pre_gain).astype(BF16)
    grad_gate = contract(normed, grads_in[:, :ff], 0, 0).astype(BF16)
    grad_up = contract(normed, grads_in[:, padded(ff) : padded(ff) + ff], 0, 0).astype(BF16)
    return (grad_hidden, grad_gate, grad_up, grad_down, grad_head, loss[0, 0])


def solution(mesh):
    return jax.shard_map(
        shards,
        mesh=mesh,
        in_specs=(
            P("vocab", "width"),
            P("width"),
            P("width"),
            P("width"),
            P("width", "vocab"),
            P("width", "vocab"),
            P("vocab", "width"),
            P("width", "vocab"),
            P(),
            P(),
        ),
        out_specs=(
            P("vocab", "width"),
            P("width", "vocab"),
            P("width", "vocab"),
            P("vocab", "width"),
            P("width", "vocab"),
            P(),
        ),
        check_vma=False,
    )
```

```python
import math

import jax
import jax.numpy as jnp
from jax import lax
from jax.experimental import pallas as pl
from jax.experimental.pallas import tpu as pltpu
from jax.sharding import PartitionSpec as P

CAP = 30.0
EPS = 1e-06
ROOT_TWO_PI = math.sqrt(2.0 / math.pi)
BF16 = jnp.bfloat16
F32 = jnp.float32
LANES = 128
CHUNK = 512


def contract(left, right, left_dim, right_dim):
    return lax.dot_general(
        left, right, (((left_dim,), (right_dim,)), ((), ())), preferred_element_type=F32
    )


def gelu_parts(value):
    square = value * value
    bent = jnp.tanh(ROOT_TWO_PI * value * (1.0 + 0.044715 * square))
    half = 0.5 * (1.0 + bent)
    slope = half + 0.5 * value * (1.0 - bent * bent) * ROOT_TWO_PI * (1.0 + 3.0 * 0.044715 * square)
    return value * half, slope


def padded(width):
    return width // LANES * LANES + LANES


def pick(tile, at):
    lane = lax.broadcasted_iota(jnp.int32, tile.shape, 1)
    return jnp.sum(jnp.where((lane == at) | (lane == at + 1), tile, 0.0), axis=1, keepdims=True)


def read_stats(tile, width, count):
    return [pick(tile, width % LANES + 2 * i) for i in range(count)]


def tail_of(width):
    return slice(width // LANES * LANES, padded(width))


def with_stats(tile, width, stats):
    lane = lax.broadcasted_iota(jnp.int32, tile.shape, 1)
    at = width % LANES
    tile = jnp.where(lane < at, tile, 0.0)
    for i, stat in enumerate(stats):
        high = stat.astype(BF16).astype(F32)
        tile = jnp.where(lane == at + 2 * i, high, tile)
        tile = jnp.where(lane == at + 2 * i + 1, stat - high, tile)
    return tile.astype(BF16)


def put(ref, block, stats):
    width = block.shape[1]
    ref[:, :width] = block
    tail = tail_of(width)
    ref[:, tail] = with_stats(ref[:, tail].astype(F32), width, stats)


def put_copies(ref, block, stats):
    put(ref.at[0], block, stats)
    whole = ref[0]
    for i in range(1, ref.shape[0]):
        ref[i] = whole


def summed(ref, columns):
    total = ref[0, :, columns].astype(F32)
    for i in range(1, ref.shape[0]):
        total = total + ref[i, :, columns].astype(F32)
    return total


def local(body, outs, *args):
    return pl.pallas_call(
        body,
        out_shape=tuple(jax.ShapeDtypeStruct(s, d) for s, d in outs),
        in_specs=[pl.BlockSpec(memory_space=pltpu.VMEM) for _ in args],
        out_specs=tuple(pl.BlockSpec(memory_space=pltpu.VMEM) for _ in outs),
        compiler_params=pltpu.CompilerParams(vmem_limit_bytes=16 << 20),
    )(*args)


def exchange(parts, axis):
    size = lax.axis_size(axis)
    if parts.ndim == 2:
        parts = parts.reshape(size, parts.shape[0] // size, parts.shape[1])
    return lax.all_to_all(parts, axis, 0, 0, tiled=True)


def flat(message):
    return message.reshape(message.shape[0] * message.shape[1], message.shape[2])


def gate_step(
    inputs, gains, gate_weight, up_weight, target_rows, ids, weights, out, *kept
):
    for source, copy in zip((target_rows, ids, weights, gains), kept):
        copy[...] = source[...]
    width = gate_weight.shape[1]
    values = inputs[...].astype(F32)
    scaled = (values * gains[0:1]).astype(BF16)
    squares = jnp.sum(values * values, axis=1, keepdims=True)
    put(out, contract(scaled, gate_weight[...], 1, 0).astype(BF16), [squares])
    out[:, padded(width) : padded(width) + width] = contract(
        scaled, up_weight[...], 1, 0
    ).astype(BF16)


def active_step(model, width, message, gate, upward, gelu_gate, gelu_slope, out):
    (squares,) = read_stats(summed(message, tail_of(width)), width, 1)
    scale = lax.rsqrt(squares / model + EPS)
    gate_value = summed(message, slice(0, width)) * scale
    up_value = summed(message, slice(padded(width), padded(width) + width)) * scale
    value, slope = gelu_parts(gate_value)
    gate[...] = gate_value
    upward[...] = up_value
    gelu_gate[...] = value
    gelu_slope[...] = slope
    put_copies(out, (value * up_value).astype(BF16), [squares])


def branch_step(message, down_weight, target_rows, out):
    width = down_weight.shape[0]
    depth = down_weight.shape[1]
    out[:, :depth] = contract(message[:, :width], down_weight[...], 1, 0).astype(BF16)
    out[:, padded(depth) : padded(depth) + depth] = target_rows[...]


def norm_step(message, inputs, gains, branch, target, out):
    width = branch.shape[1]
    value = summed(message, slice(0, width))
    branch[...] = value
    target[...] = summed(message, slice(padded(width), padded(width) + width))
    bent = value * gains[1:2]
    own = inputs[...].astype(F32)
    stats = [
        jnp.sum(x, axis=1, keepdims=True) for x in (value * value, own * bent, bent * bent, own * own)
    ]
    lane = lax.broadcasted_iota(jnp.int32, out.shape[1:], 1)
    tile = jnp.zeros(out.shape[1:], F32)
    for i, stat in enumerate(stats):
        tile = jnp.where(lane == i, stat, tile)
    for i in range(out.shape[0]):
        out[i] = tile


def scale_step(model, message, branch, scales, out):
    tile = message[0]
    for i in range(1, message.shape[0]):
        tile = tile + message[i]
    lane = lax.broadcasted_iota(jnp.int32, tile.shape, 1)
    square, cross, bent, own = [
        jnp.sum(jnp.where(lane == i, tile, 0.0), axis=1, keepdims=True) for i in range(4)
    ]
    post = lax.rsqrt(square / model + EPS)
    final_squares = own + post * (2.0 * cross + post * bent)
    final = lax.rsqrt(jnp.maximum(final_squares, 0.0) / model + EPS)
    pre = lax.rsqrt(own / model + EPS)
    scales[...] = jnp.where(lane == 0, post, jnp.where(lane == 1, final, pre))
    put_copies(out, branch[...].astype(BF16), [post, final])


def logit_step(copies_n, message, inputs, gains, down_weight, head, out, final):
    width = final.shape[1]
    branch = message[:, :width]
    post, scale = read_stats(message[:, tail_of(width)].astype(F32), width, 2)
    resid = inputs[...].astype(F32) + branch.astype(F32) * post * gains[1:2]
    final[...] = (resid * scale * gains[2:3]).astype(BF16)
    vocab = head.shape[1]
    hidden = down_weight.shape[0]
    out[:, vocab : vocab + hidden] = contract(branch, down_weight[...], 1, 1).astype(BF16)
    tail = tail_of(vocab + hidden)
    out[:, tail] = with_stats(out[:, tail].astype(F32), vocab + hidden, [post / copies_n])
    for i in range(0, vocab, CHUNK):
        columns = slice(i, i + CHUNK)
        out[:, columns] = contract(final[...], head[:, columns], 1, 0).astype(BF16)


def soft_step(vocab, hidden, message, ids, out, branch_down):
    rows = message.shape[1]
    step = 256
    others = jnp.zeros((rows, step), F32)
    cross = jnp.zeros((rows, step), F32)
    target = jnp.zeros((rows, step), F32)
    lane = lax.broadcasted_iota(jnp.int32, (rows, step), 1)
    for i in range(vocab // step):
        columns = slice(i * step, (i + 1) * step)
        logits = summed(message, columns)
        hits = lane == ids[...] - i * step
        bent = jnp.tanh(logits / CAP)
        raised = jnp.where(hits, 0.0, jnp.exp(CAP * bent - CAP))
        sloped = raised * (1.0 - bent * bent)
        others = others + raised
        cross = cross + sloped * logits
        target = target + jnp.where(hits, logits, 0.0)
        part = sloped.astype(BF16)
        for j in range(out.shape[0]):
            out[j, :, columns] = part
    stats = [jnp.sum(x, axis=1, keepdims=True) for x in (others, cross, target)]
    tile = with_stats(jnp.zeros((rows, LANES), F32), vocab, stats)
    for j in range(out.shape[0]):
        out[j, :, vocab : vocab + LANES] = tile
    branch_down[...] = summed(message, slice(vocab, vocab + padded(hidden)))


def row_step(message, head, out):
    vocab = head.shape[1]
    total = contract(message[:, :vocab], head[...], 1, 1)
    put(
        out,
        total.astype(BF16),
        read_stats(message[:, vocab : vocab + LANES].astype(F32), vocab, 3),
    )


def resid_step(
    model, message, target_rows, branch, inputs, scales, weights, gains, grad_resid, out
):
    width = branch.shape[1]
    others, cross, logit = read_stats(summed(message, tail_of(width)), width, 3)
    bent = jnp.tanh(logit / CAP)
    target = CAP * bent
    total = others + jnp.exp(target - CAP)
    logprob = target - CAP - jnp.log(total)
    spread = weights[...] / total
    pull = -spread * others * (1.0 - bent * bent)
    post = scales[:, 0:1]
    final = scales[:, 1:2]
    post_gain = gains[1:2]
    final_gain = gains[2:3]
    grad_final = spread * summed(message, slice(0, width)) + pull * target_rows[...]
    back_final = (spread * cross + pull * logit) / final
    value = branch[...]
    resid = inputs[...].astype(F32) + post * value * post_gain
    grad = final * grad_final * final_gain - resid * (
        final * final * final * back_final / model
    )
    grad_resid[...] = grad
    weighted = grad * post_gain
    back_post = jnp.sum(weighted * value, axis=1, keepdims=True)
    put_copies(
        out,
        (post * weighted).astype(BF16),
        [spread, pull, weights[...] * logprob, back_post],
    )


def down_step(message, down_weight, out, loss):
    width = down_weight.shape[1]
    _, _, score, back_post = read_stats(message[:, tail_of(width)].astype(F32), width, 4)
    put(
        out,
        contract(message[:, :width], down_weight[...], 1, 1).astype(BF16),
        [back_post],
    )
    loss[...] = -jnp.sum(score, axis=0, keepdims=True) / message.shape[0]


def hidden_step(model, message, branch_down, gate, upward, gelu_gate, gelu_slope, out):
    rows, width = gate.shape
    (back_post,) = read_stats(summed(message, tail_of(width)), width, 1)
    (post,) = read_stats(branch_down[:, tail_of(width)], width, 1)
    grad = summed(message, slice(0, width)) - branch_down[:, :width] * (
        post * post * post * back_post / model
    )
    gate_in = (grad * upward[...] * gelu_slope[...]).astype(BF16)
    up_in = (grad * gelu_gate[...]).astype(BF16)
    back = jnp.sum(
        gate_in.astype(F32) * gate[...] + up_in.astype(F32) * upward[...], axis=1, keepdims=True
    )
    start = padded(width)
    put(out.at[0], gate_in, [back, back_post])
    out[0, :, start : start + width] = up_in
    whole = out[0]
    for i in range(1, out.shape[0]):
        out[i] = whole


def normed_step(model, message, gate_weight, up_weight, active, branch, weighted, out, rates):
    width, hidden = gate_weight.shape
    start = padded(hidden)
    total = contract(message[:, :hidden], gate_weight[...], 1, 1) + contract(
        message[:, start : start + hidden], up_weight[...], 1, 1
    )
    back, back_post = read_stats(message[:, tail_of(hidden)].astype(F32), hidden, 2)
    put(out, total.astype(BF16), [back])
    (squares,) = read_stats(active[:, tail_of(hidden)].astype(F32), hidden, 1)
    (post,) = read_stats(branch[:, tail_of(width)].astype(F32), width, 1)
    spread, pull = read_stats(weighted[:, tail_of(width)].astype(F32), width, 2)
    lane = lax.broadcasted_iota(jnp.int32, rates.shape, 1)
    tile = jnp.where(lane == 0, spread, pull)
    tile = jnp.where(lane == 2, post * post * post * back_post / model, tile)
    rates[...] = jnp.where(lane == 3, lax.rsqrt(squares / model + EPS), tile)


def last_step(model, message, grad_resid, inputs, scales, gains, out):
    width = out.shape[1]
    scale = scales[:, 2:3]
    (back,) = read_stats(summed(message, tail_of(width)), width, 1)
    weighted = summed(message, slice(0, width)) * gains[0:1]
    out[...] = (
        grad_resid[...] + scale * weighted - inputs[...].astype(F32) * (scale * scale * back / model)
    ).astype(BF16)


def shards(
    hidden,
    pre_gain,
    post_gain,
    final_gain,
    gate_weight,
    up_weight,
    down_weight,
    head_weight,
    token_ids,
    rewards,
):
    tok_dev, width = hidden.shape
    tokens = token_ids.shape[0]
    rows_n = lax.axis_size("vocab")
    cols_n = lax.axis_size("width")
    model = width * cols_n
    ff = gate_weight.shape[1]
    vocab = head_weight.shape[1]
    sub = tokens // cols_n
    vocab_index = lax.axis_index("vocab")
    width_index = lax.axis_index("width")
    gains = jnp.stack([pre_gain, post_gain, final_gain])

    weights = jnp.repeat(rewards, tokens // rewards.shape[0])
    own_weights = lax.dynamic_slice_in_dim(weights, vocab_index * tok_dev, tok_dev, 0)[:, None]
    ids = token_ids - vocab_index * vocab
    hits = jnp.arange(vocab, dtype=jnp.int32)[None, :] == ids[:, None]
    sub_ids = lax.dynamic_slice_in_dim(ids, width_index * sub, sub, 0)[:, None]
    target_part = contract(hits.astype(BF16), head_weight, 1, 1).astype(BF16)
    inputs = flat(exchange(jnp.broadcast_to(hidden[None], (rows_n, tok_dev, width)), "vocab"))
    message, target_part, sub_ids, own_weights, gains = local(
        gate_step,
        [
            ((tokens, padded(ff) * 2), BF16),
            ((tokens, width), BF16),
            ((sub, 1), jnp.int32),
            ((tok_dev, 1), F32),
            ((3, width), F32),
        ],
        inputs,
        gains,
        gate_weight,
        up_weight,
        target_part,
        sub_ids,
        own_weights,
    )
    gate, upward, gelu_gate, gelu_slope, message = local(
        lambda *refs: active_step(model, ff, *refs),
        [((sub, ff), F32)] * 4 + [((cols_n, sub, padded(ff)), BF16)],
        exchange(message, "width"),
    )
    active = flat(exchange(message, "width"))
    (message,) = local(
        branch_step, [((tokens, padded(width) * 2), BF16)], active, down_weight, target_part
    )
    branch, target_rows, message = local(
        norm_step,
        [((tok_dev, width), F32)] * 2 + [((cols_n, tok_dev, LANES), F32)],
        exchange(message, "vocab"),
        hidden,
        gains,
    )
    scales, message = local(
        lambda *refs: scale_step(model, *refs),
        [((tok_dev, LANES), F32), ((rows_n, tok_dev, padded(width)), BF16)],
        exchange(message, "width"),
        branch,
    )
    branch_all = flat(exchange(message, "vocab"))
    message, final = local(
        lambda *refs: logit_step(cols_n, *refs),
        [((tokens, vocab + padded(ff)), BF16), ((tokens, width), BF16)],
        branch_all,
        inputs,
        gains,
        down_weight,
        head_weight,
    )
    message, branch_down = local(
        lambda *refs: soft_step(vocab, ff, *refs),
        [((cols_n, sub, vocab + LANES), BF16), ((sub, padded(ff)), F32)],
        exchange(message, "width"),
        sub_ids,
    )
    sloped = flat(exchange(message, "width"))
    (message,) = local(
        row_step,
        [((tokens, padded(width)), BF16)],
        sloped,
        head_weight,
    )
    grad_resid, message = local(
        lambda *refs: resid_step(model, *refs),
        [((tok_dev, width), F32), ((rows_n, tok_dev, padded(width)), BF16)],
        exchange(message, "vocab"),
        target_rows,
        branch,
        hidden,
        scales,
        own_weights,
        gains,
    )
    weighted = flat(exchange(message, "vocab"))
    message, loss = local(
        down_step,
        [((tokens, padded(ff)), BF16), ((1, 1), F32)],
        weighted,
        down_weight,
    )
    (message,) = local(
        lambda *refs: hidden_step(model, *refs),
        [((cols_n, sub, padded(ff) * 2), BF16)],
        exchange(message, "width"),
        branch_down,
        gate,
        upward,
        gelu_gate,
        gelu_slope,
    )
    grads_in = flat(exchange(message, "width"))
    message, rates = local(
        lambda *refs: normed_step(model, *refs),
        [((tokens, padded(width)), BF16), ((tokens, LANES), F32)],
        grads_in,
        gate_weight,
        up_weight,
        active,
        branch_all,
        weighted,
    )
    (grad_hidden,) = local(
        lambda *refs: last_step(model, *refs),
        [((tok_dev, width), BF16)],
        exchange(message, "vocab"),
        grad_resid,
        hidden,
        scales,
        gains,
    )

    spread, pull, along, scale_pre = [rates[:, i : i + 1] for i in range(4)]
    delta = (spread * sloped[:, :vocab].astype(F32) + jnp.where(hits, pull, 0.0)).astype(BF16)
    grad_head = contract(final, delta, 0, 0).astype(BF16)
    grad_branch = (
        weighted[:, :width].astype(F32) - branch_all[:, :width].astype(F32) * along
    ).astype(BF16)
    grad_down = contract(active[:, :ff], grad_branch, 0, 0).astype(BF16)
    normed = (inputs.astype(F32) * scale_pre * pre_gain).astype(BF16)
    grad_gate = contract(normed, grads_in[:, :ff], 0, 0).astype(BF16)
    grad_up = contract(normed, grads_in[:, padded(ff) : padded(ff) + ff], 0, 0).astype(BF16)
    return (grad_hidden, grad_gate, grad_up, grad_down, grad_head, loss[0, 0])


def solution(mesh):
    return jax.shard_map(
        shards,
        mesh=mesh,
        in_specs=(
            P("vocab", "width"),
            P("width"),
            P("width"),
            P("width"),
            P("width", "vocab"),
            P("width", "vocab"),
            P("vocab", "width"),
            P("width", "vocab"),
            P(),
            P(),
        ),
        out_specs=(
            P("vocab", "width"),
            P("width", "vocab"),
            P("width", "vocab"),
            P("vocab", "width"),
            P("width", "vocab"),
            P(),
        ),
        check_vma=False,
    )
```

```python
import math

import jax
import jax.numpy as jnp
from jax import lax
from jax.experimental import pallas as pl
from jax.experimental.pallas import tpu as pltpu
from jax.sharding import Mesh
from jax.sharding import PartitionSpec as P

CAP = 30.0
EPS = 1e-06
ROOT_TWO_PI = math.sqrt(2.0 / math.pi)
BF16 = jnp.bfloat16
F32 = jnp.float32
LANES = 128
CHUNK = 512


def contract(left, right, left_dim, right_dim):
    return lax.dot_general(
        left, right, (((left_dim,), (right_dim,)), ((), ())), preferred_element_type=F32
    )


def gelu_parts(value):
    square = value * value
    bent = jnp.tanh(ROOT_TWO_PI * value * (1.0 + 0.044715 * square))
    half = 0.5 * (1.0 + bent)
    slope = half + 0.5 * value * (1.0 - bent * bent) * ROOT_TWO_PI * (1.0 + 3.0 * 0.044715 * square)
    return value * half, slope


def padded(width):
    return width // LANES * LANES + LANES


def pick(tile, at):
    lane = lax.broadcasted_iota(jnp.int32, tile.shape, 1)
    return jnp.sum(jnp.where((lane == at) | (lane == at + 1), tile, 0.0), axis=1, keepdims=True)


def read_stats(tile, width, count):
    return [pick(tile, width % LANES + 2 * i) for i in range(count)]


def tail_of(width):
    return slice(width // LANES * LANES, padded(width))


def with_stats(tile, width, stats):
    lane = lax.broadcasted_iota(jnp.int32, tile.shape, 1)
    at = width % LANES
    tile = jnp.where(lane < at, tile, 0.0)
    for i, stat in enumerate(stats):
        high = stat.astype(BF16).astype(F32)
        tile = jnp.where(lane == at + 2 * i, high, tile)
        tile = jnp.where(lane == at + 2 * i + 1, stat - high, tile)
    return tile


def put(ref, block, stats):
    width = block.shape[1]
    ref[:, :width] = block
    tail = tail_of(width)
    ref[:, tail] = with_stats(ref[:, tail].astype(F32), width, stats).astype(ref.dtype)


def put_halves(mine, theirs, block, stats):
    half = mine.shape[0]
    put(mine, block[:half], [stat[:half] for stat in stats])
    put(theirs, block[half:].astype(BF16), [stat[half:] for stat in stats])


def put_copies(ref, block, stats):
    put(ref.at[0], block, stats)
    whole = ref[0]
    for i in range(1, ref.shape[0]):
        ref[i] = whole


def summed(ref, columns):
    total = ref[0, :, columns].astype(F32)
    for i in range(1, ref.shape[0]):
        total = total + ref[i, :, columns].astype(F32)
    return total


def local(body, outs, *args, hbm=(), scratch=()):
    return pl.pallas_call(
        body,
        out_shape=tuple(jax.ShapeDtypeStruct(s, d) for s, d in outs),
        in_specs=[
            pl.BlockSpec(memory_space=pltpu.HBM if i in hbm else pltpu.VMEM)
            for i in range(len(args))
        ],
        out_specs=tuple(pl.BlockSpec(memory_space=pltpu.VMEM) for _ in outs),
        scratch_shapes=scratch,
        compiler_params=pltpu.CompilerParams(vmem_limit_bytes=16 << 20),
    )(*args)


def exchange(parts, axis):
    size = lax.axis_size(axis)
    if parts.ndim == 2:
        parts = parts.reshape(size, parts.shape[0] // size, parts.shape[1])
    return lax.all_to_all(parts, axis, 0, 0, tiled=True)


def flat(message):
    return message.reshape(message.shape[0] * message.shape[1], message.shape[2])


def rejoin(near, far, whole):
    half = near.shape[0]
    whole[:half] = near[...]
    whole[half:] = far[...]


def pair_step(width, count, mine, theirs, *rest):
    *held, out = rest
    for source, copy in zip(held[: len(held) // 2], held[len(held) // 2 :]):
        copy[...] = source[...]
    out[...] = (mine[...] + theirs[...].astype(F32)).astype(BF16)
    if count:
        tail = tail_of(width)
        tile = mine[:, tail] + theirs[:, tail].astype(F32)
        out[:, tail] = with_stats(tile, width, read_stats(tile, width, count)).astype(BF16)


def swap(values):
    return lax.ppermute(values, "core", [(0, 1), (1, 0)])


def gathered(copies):
    near = flat(exchange(copies, "rows"))
    return near, swap(near)


def reduced(mine, theirs, width, count, *held):
    *held, message = local(
        lambda *refs: pair_step(width, count, *refs),
        [*((x.shape, x.dtype) for x in held), (mine.shape, BF16)],
        mine,
        swap(theirs),
        *held,
    )
    return (exchange(message, "rows"), *held)


def gate_step(
    near, far, gains, gate_weight, up_weight, target_rows, ids, weights, out, inputs, *kept
):
    rejoin(near, far, inputs)
    for source, copy in zip((target_rows, ids, weights, gains), kept):
        copy[...] = source[...]
    width = gate_weight.shape[1]
    values = inputs[...].astype(F32)
    scaled = (values * gains[0:1]).astype(BF16)
    squares = jnp.sum(values * values, axis=1, keepdims=True)
    put(out, contract(scaled, gate_weight[...], 1, 0).astype(BF16), [squares])
    out[:, padded(width) : padded(width) + width] = contract(
        scaled, up_weight[...], 1, 0
    ).astype(BF16)


def active_step(model, width, message, gate, upward, gelu_gate, gelu_slope, out):
    (squares,) = read_stats(summed(message, tail_of(width)), width, 1)
    scale = lax.rsqrt(squares / model + EPS)
    gate_value = summed(message, slice(0, width)) * scale
    up_value = summed(message, slice(padded(width), padded(width) + width)) * scale
    value, slope = gelu_parts(gate_value)
    gate[...] = gate_value
    upward[...] = up_value
    gelu_gate[...] = value
    gelu_slope[...] = slope
    put_copies(out, (value * up_value).astype(BF16), [squares])


def branch_step(message, down_weight, target_rows, mine, theirs):
    hidden, width = down_weight.shape
    half = mine.shape[0]
    block = contract(message[:, :hidden], down_weight[...], 1, 0)
    mine[:, :width] = block[:half]
    theirs[:, :width] = block[half:].astype(BF16)
    mine[:, width : 2 * width] = target_rows[:half].astype(F32)
    theirs[:, width : 2 * width] = target_rows[half:]


def norm_step(message, inputs, gains, branch, target, out):
    width = branch.shape[1]
    both = summed(message, slice(0, 2 * width))
    value = both[:, :width]
    branch[...] = value
    target[...] = both[:, width:]
    bent = value * gains[1:2]
    own = inputs[...].astype(F32)
    stats = [
        jnp.sum(x, axis=1, keepdims=True) for x in (value * value, own * bent, bent * bent, own * own)
    ]
    lane = lax.broadcasted_iota(jnp.int32, out.shape[1:], 1)
    tile = jnp.zeros(out.shape[1:], F32)
    for i, stat in enumerate(stats):
        tile = jnp.where(lane == i, stat, tile)
    for i in range(out.shape[0]):
        out[i] = tile


def scale_step(model, message, branch, scales, out):
    tile = message[0]
    for i in range(1, message.shape[0]):
        tile = tile + message[i]
    lane = lax.broadcasted_iota(jnp.int32, tile.shape, 1)
    square, cross, bent, own = [
        jnp.sum(jnp.where(lane == i, tile, 0.0), axis=1, keepdims=True) for i in range(4)
    ]
    post = lax.rsqrt(square / model + EPS)
    final_squares = own + post * (2.0 * cross + post * bent)
    final = lax.rsqrt(jnp.maximum(final_squares, 0.0) / model + EPS)
    pre = lax.rsqrt(own / model + EPS)
    scales[...] = jnp.where(lane == 0, post, jnp.where(lane == 1, final, pre))
    put_copies(out, branch[...].astype(BF16), [post, final])


def logit_step(
    copies_n, near, far, inputs, gains, down_weight, head, out, final, message, buffer, sems
):
    vocab = head.shape[1]
    copies = [
        pltpu.make_async_copy(head.at[:, pl.ds(i * CHUNK, CHUNK)], buffer.at[i], sems.at[i])
        for i in range(vocab // CHUNK)
    ]
    for copy in copies:
        copy.start()
    rejoin(near, far, message)
    width = final.shape[1]
    branch = message[:, :width]
    post, scale = read_stats(message[:, tail_of(width)].astype(F32), width, 2)
    resid = inputs[...].astype(F32) + branch.astype(F32) * post * gains[1:2]
    final[...] = (resid * scale * gains[2:3]).astype(BF16)
    hidden = down_weight.shape[0]
    out[:, vocab : vocab + hidden] = contract(branch, down_weight[...], 1, 1).astype(BF16)
    tail = tail_of(vocab + hidden)
    tile = with_stats(out[:, tail].astype(F32), vocab + hidden, [post / copies_n])
    out[:, tail] = tile.astype(BF16)
    for i, copy in enumerate(copies):
        copy.wait()
        columns = slice(i * CHUNK, (i + 1) * CHUNK)
        out[:, columns] = contract(final[...], buffer[i], 1, 0).astype(BF16)


def soft_step(vocab, hidden, message, ids, out, branch_down):
    rows = message.shape[1]
    step = 256
    others = jnp.zeros((rows, step), F32)
    cross = jnp.zeros((rows, step), F32)
    target = jnp.zeros((rows, step), F32)
    lane = lax.broadcasted_iota(jnp.int32, (rows, step), 1)
    for i in range(vocab // step):
        columns = slice(i * step, (i + 1) * step)
        logits = summed(message, columns)
        hits = lane == ids[...] - i * step
        bent = jnp.tanh(logits / CAP)
        raised = jnp.where(hits, 0.0, jnp.exp(CAP * bent - CAP))
        sloped = raised * (1.0 - bent * bent)
        others = others + raised
        cross = cross + sloped * logits
        target = target + jnp.where(hits, logits, 0.0)
        part = sloped.astype(BF16)
        for j in range(out.shape[0]):
            out[j, :, columns] = part
    stats = [jnp.sum(x, axis=1, keepdims=True) for x in (others, cross, target)]
    tile = with_stats(jnp.zeros((rows, LANES), F32), vocab, stats).astype(BF16)
    for j in range(out.shape[0]):
        out[j, :, vocab : vocab + LANES] = tile
    branch_down[...] = summed(message, slice(vocab, vocab + padded(hidden)))


def row_step(message, head, mine, theirs):
    vocab = head.shape[1]
    total = contract(message[:, :vocab], head[...], 1, 1)
    stats = read_stats(message[:, vocab : vocab + LANES].astype(F32), vocab, 3)
    put_halves(mine, theirs, total, stats)


def resid_step(
    model, message, target_rows, branch, inputs, scales, weights, gains, grad_resid, out
):
    width = branch.shape[1]
    others, cross, logit = read_stats(summed(message, tail_of(width)), width, 3)
    bent = jnp.tanh(logit / CAP)
    target = CAP * bent
    total = others + jnp.exp(target - CAP)
    logprob = target - CAP - jnp.log(total)
    spread = weights[...] / total
    pull = -spread * others * (1.0 - bent * bent)
    post = scales[:, 0:1]
    final = scales[:, 1:2]
    post_gain = gains[1:2]
    final_gain = gains[2:3]
    grad_final = spread * summed(message, slice(0, width)) + pull * target_rows[...]
    back_final = (spread * cross + pull * logit) / final
    value = branch[...]
    resid = inputs[...].astype(F32) + post * value * post_gain
    grad = final * grad_final * final_gain - resid * (
        final * final * final * back_final / model
    )
    grad_resid[...] = grad
    weighted = grad * post_gain
    back_post = jnp.sum(weighted * value, axis=1, keepdims=True)
    put_copies(
        out,
        (post * weighted).astype(BF16),
        [spread, pull, weights[...] * logprob, back_post],
    )


def down_step(near, far, down_weight, out, message, loss):
    rejoin(near, far, message)
    width = down_weight.shape[1]
    _, _, score, back_post = read_stats(message[:, tail_of(width)].astype(F32), width, 4)
    put(
        out,
        contract(message[:, :width], down_weight[...], 1, 1).astype(BF16),
        [back_post],
    )
    loss[...] = -jnp.sum(score, axis=0, keepdims=True) / message.shape[0]


def hidden_step(model, message, branch_down, gate, upward, gelu_gate, gelu_slope, out):
    rows, width = gate.shape
    (back_post,) = read_stats(summed(message, tail_of(width)), width, 1)
    (post,) = read_stats(branch_down[:, tail_of(width)], width, 1)
    grad = summed(message, slice(0, width)) - branch_down[:, :width] * (
        post * post * post * back_post / model
    )
    gate_in = (grad * upward[...] * gelu_slope[...]).astype(BF16)
    up_in = (grad * gelu_gate[...]).astype(BF16)
    back = jnp.sum(
        gate_in.astype(F32) * gate[...] + up_in.astype(F32) * upward[...], axis=1, keepdims=True
    )
    start = padded(width)
    put(out.at[0], gate_in, [back, back_post])
    out[0, :, start : start + width] = up_in
    whole = out[0]
    for i in range(1, out.shape[0]):
        out[i] = whole


def normed_step(
    model, message, gate_weight, up_weight, active, branch, weighted, mine, theirs, rates
):
    width, hidden = gate_weight.shape
    start = padded(hidden)
    total = contract(message[:, :hidden], gate_weight[...], 1, 1) + contract(
        message[:, start : start + hidden], up_weight[...], 1, 1
    )
    back, back_post = read_stats(message[:, tail_of(hidden)].astype(F32), hidden, 2)
    put_halves(mine, theirs, total, [back])
    (squares,) = read_stats(active[:, tail_of(hidden)].astype(F32), hidden, 1)
    (post,) = read_stats(branch[:, tail_of(width)].astype(F32), width, 1)
    spread, pull = read_stats(weighted[:, tail_of(width)].astype(F32), width, 2)
    lane = lax.broadcasted_iota(jnp.int32, rates.shape, 1)
    tile = jnp.where(lane == 0, spread, pull)
    tile = jnp.where(lane == 2, post * post * post * back_post / model, tile)
    rates[...] = jnp.where(lane == 3, lax.rsqrt(squares / model + EPS), tile)


def last_step(model, message, grad_resid, inputs, scales, gains, out):
    width = out.shape[1]
    scale = scales[:, 2:3]
    (back,) = read_stats(summed(message, tail_of(width)), width, 1)
    weighted = summed(message, slice(0, width)) * gains[0:1]
    out[...] = (
        grad_resid[...] + scale * weighted - inputs[...].astype(F32) * (scale * scale * back / model)
    ).astype(BF16)


def shards(
    hidden,
    pre_gain,
    post_gain,
    final_gain,
    gate_weight,
    up_weight,
    down_weight,
    head_weight,
    token_ids,
    rewards,
):
    tok_dev, width = hidden.shape
    tokens = token_ids.shape[0]
    rows_n = lax.axis_size("rows")
    cols_n = lax.axis_size("width")
    model = width * cols_n
    ff = gate_weight.shape[1]
    vocab = head_weight.shape[1]
    sub = tokens // cols_n
    half = tokens // 2
    core = lax.axis_index("core")
    vocab_index = lax.axis_index("rows") * 2 + core
    width_index = lax.axis_index("width")
    gains = jnp.stack([pre_gain, post_gain, final_gain])

    weights = jnp.repeat(rewards, tokens // rewards.shape[0])
    own_weights = lax.dynamic_slice_in_dim(weights, vocab_index * tok_dev, tok_dev, 0)[:, None]
    ids = token_ids.reshape(rows_n, 2, tok_dev)
    ids = jnp.where(core == 0, jnp.swapaxes(ids, 0, 1), jnp.swapaxes(ids[:, ::-1], 0, 1))
    ids = ids.reshape(tokens) - vocab_index * vocab
    hits = jnp.arange(vocab, dtype=jnp.int32)[None, :] == ids[:, None]
    sub_ids = lax.dynamic_slice_in_dim(ids, width_index * sub, sub, 0)[:, None]
    target_part = contract(hits.astype(BF16), head_weight, 1, 1).astype(BF16)
    near, far = gathered(jnp.broadcast_to(hidden[None], (rows_n, tok_dev, width)))
    message, inputs, target_part, sub_ids, own_weights, gains = local(
        gate_step,
        [
            ((tokens, padded(ff) * 2), BF16),
            ((tokens, width), BF16),
            ((tokens, width), BF16),
            ((sub, 1), jnp.int32),
            ((tok_dev, 1), F32),
            ((3, width), F32),
        ],
        near,
        far,
        gains,
        gate_weight,
        up_weight,
        target_part,
        sub_ids,
        own_weights,
    )
    gate, upward, gelu_gate, gelu_slope, message = local(
        lambda *refs: active_step(model, ff, *refs),
        [((sub, ff), F32)] * 4 + [((cols_n, sub, padded(ff)), BF16)],
        exchange(message, "width"),
    )
    active = flat(exchange(message, "width"))
    mine, theirs = local(
        branch_step,
        [((half, width * 2), F32), ((half, width * 2), BF16)],
        active,
        down_weight,
        target_part,
    )
    branch, target_rows, message = local(
        norm_step,
        [((tok_dev, width), F32)] * 2 + [((cols_n, tok_dev, LANES), F32)],
        *reduced(mine, theirs, width * 2, 0),
        hidden,
        gains,
    )
    scales, message = local(
        lambda *refs: scale_step(model, *refs),
        [((tok_dev, LANES), F32), ((rows_n, tok_dev, padded(width)), BF16)],
        exchange(message, "width"),
        branch,
    )
    near, far = gathered(message)
    message, final, branch_all = local(
        lambda *refs: logit_step(cols_n, *refs),
        [
            ((tokens, vocab + padded(ff)), BF16),
            ((tokens, width), BF16),
            ((tokens, padded(width)), BF16),
        ],
        near,
        far,
        inputs,
        gains,
        down_weight,
        pltpu.with_memory_space_constraint(head_weight, pltpu.HBM),
        hbm=(5,),
        scratch=(
            pltpu.VMEM((vocab // CHUNK, width, CHUNK), BF16),
            pltpu.SemaphoreType.DMA((vocab // CHUNK,)),
        ),
    )
    message, branch_down = local(
        lambda *refs: soft_step(vocab, ff, *refs),
        [((cols_n, sub, vocab + LANES), BF16), ((sub, padded(ff)), F32)],
        exchange(message, "width"),
        sub_ids,
    )
    sloped = flat(exchange(message, "width"))
    halves = [((half, padded(width)), F32), ((half, padded(width)), BF16)]
    mine, theirs = local(row_step, halves, sloped, head_weight)
    grad_resid, message = local(
        lambda *refs: resid_step(model, *refs),
        [((tok_dev, width), F32), ((rows_n, tok_dev, padded(width)), BF16)],
        *reduced(mine, theirs, width, 3),
        target_rows,
        branch,
        hidden,
        scales,
        own_weights,
        gains,
    )
    near, far = gathered(message)
    message, weighted, loss = local(
        down_step,
        [((tokens, padded(ff)), BF16), ((tokens, padded(width)), BF16), ((1, 1), F32)],
        near,
        far,
        down_weight,
    )
    (message,) = local(
        lambda *refs: hidden_step(model, *refs),
        [((cols_n, sub, padded(ff) * 2), BF16)],
        exchange(message, "width"),
        branch_down,
        gate,
        upward,
        gelu_gate,
        gelu_slope,
    )
    grads_in = flat(exchange(message, "width"))
    mine, theirs, rates = local(
        lambda *refs: normed_step(model, *refs),
        [*halves, ((tokens, LANES), F32)],
        grads_in,
        gate_weight,
        up_weight,
        active,
        branch_all,
        weighted,
    )
    message, rates = reduced(mine, theirs, width, 1, rates)
    (grad_hidden,) = local(
        lambda *refs: last_step(model, *refs),
        [((tok_dev, width), BF16)],
        message,
        grad_resid,
        hidden,
        scales,
        gains,
    )

    spread, pull, along, scale_pre = [rates[:, i : i + 1] for i in range(4)]
    delta = (spread * sloped[:, :vocab].astype(F32) + jnp.where(hits, pull, 0.0)).astype(BF16)
    grad_head = contract(final, delta, 0, 0).astype(BF16)
    grad_branch = (
        weighted[:, :width].astype(F32) - branch_all[:, :width].astype(F32) * along
    ).astype(BF16)
    grad_down = contract(active[:, :ff], grad_branch, 0, 0).astype(BF16)
    normed = (inputs.astype(F32) * scale_pre * pre_gain).astype(BF16)
    grad_gate = contract(normed, grads_in[:, :ff], 0, 0).astype(BF16)
    grad_up = contract(normed, grads_in[:, padded(ff) : padded(ff) + ff], 0, 0).astype(BF16)
    return (grad_hidden, grad_gate, grad_up, grad_down, grad_head, loss[0, 0])


def solution(mesh):
    devices = mesh.devices
    vocab = ("rows", "core")
    return jax.shard_map(
        shards,
        mesh=Mesh(
            devices.reshape(devices.shape[0] // 2, 2, devices.shape[1]), (*vocab, "width")
        ),
        in_specs=(
            P(vocab, "width"),
            P("width"),
            P("width"),
            P("width"),
            P("width", vocab),
            P("width", vocab),
            P(vocab, "width"),
            P("width", vocab),
            P(),
            P(),
        ),
        out_specs=(
            P(vocab, "width"),
            P("width", vocab),
            P("width", vocab),
            P(vocab, "width"),
            P("width", vocab),
            P(),
        ),
        check_vma=False,
    )
```

```python
import math

import jax
import jax.numpy as jnp
from jax import lax
from jax.experimental import pallas as pl
from jax.experimental.pallas import tpu as pltpu
from jax.sharding import Mesh
from jax.sharding import PartitionSpec as P

CAP = 30.0
EPS = 1e-06
ROOT_TWO_PI = math.sqrt(2.0 / math.pi)
BF16 = jnp.bfloat16
F32 = jnp.float32
LANES = 128
CHUNK = 512


def contract(left, right, left_dim, right_dim):
    return lax.dot_general(
        left, right, (((left_dim,), (right_dim,)), ((), ())), preferred_element_type=F32
    )


def gelu_parts(value):
    square = value * value
    bent = jnp.tanh(ROOT_TWO_PI * value * (1.0 + 0.044715 * square))
    half = 0.5 * (1.0 + bent)
    slope = half + 0.5 * value * (1.0 - bent * bent) * ROOT_TWO_PI * (1.0 + 3.0 * 0.044715 * square)
    return value * half, slope


def padded(width):
    return width // LANES * LANES + LANES


def pick(tile, at):
    lane = lax.broadcasted_iota(jnp.int32, tile.shape, 1)
    return jnp.sum(jnp.where((lane == at) | (lane == at + 1), tile, 0.0), axis=1, keepdims=True)


def read_stats(tile, width, count):
    return [pick(tile, width % LANES + 2 * i) for i in range(count)]


def tail_of(width):
    return slice(width // LANES * LANES, padded(width))


def with_stats(tile, width, stats):
    lane = lax.broadcasted_iota(jnp.int32, tile.shape, 1)
    at = width % LANES
    tile = jnp.where(lane < at, tile, 0.0)
    for i, stat in enumerate(stats):
        high = stat.astype(BF16).astype(F32)
        tile = jnp.where(lane == at + 2 * i, high, tile)
        tile = jnp.where(lane == at + 2 * i + 1, stat - high, tile)
    return tile


def put(ref, block, stats):
    width = block.shape[1]
    ref[:, :width] = block
    tail = tail_of(width)
    ref[:, tail] = with_stats(ref[:, tail].astype(F32), width, stats).astype(ref.dtype)


def put_halves(mine, theirs, block, stats):
    half = mine.shape[0]
    put(mine, block[:half], [stat[:half] for stat in stats])
    put(theirs, block[half:].astype(BF16), [stat[half:] for stat in stats])


def put_copies(ref, block, stats):
    put(ref.at[0], block, stats)
    whole = ref[0]
    for i in range(1, ref.shape[0]):
        ref[i] = whole


def summed(ref, columns):
    total = ref[0, :, columns].astype(F32)
    for i in range(1, ref.shape[0]):
        total = total + ref[i, :, columns].astype(F32)
    return total


def local(body, outs, *args, off_chip=(), scratch=()):
    return pl.pallas_call(
        body,
        out_shape=tuple(jax.ShapeDtypeStruct(s, d) for s, d in outs),
        in_specs=[pl.BlockSpec(memory_space=pltpu.VMEM) for _ in args],
        out_specs=tuple(
            pl.BlockSpec(memory_space=pltpu.HBM if i in off_chip else pltpu.VMEM)
            for i in range(len(outs))
        ),
        scratch_shapes=scratch,
        compiler_params=pltpu.CompilerParams(vmem_limit_bytes=16 << 20),
    )(*args)


def exchange(parts, axis):
    size = lax.axis_size(axis)
    if parts.ndim == 2:
        parts = parts.reshape(size, parts.shape[0] // size, parts.shape[1])
    return lax.all_to_all(parts, axis, 0, 0, tiled=True)


def flat(message):
    return message.reshape(message.shape[0] * message.shape[1], message.shape[2])


def rejoin(near, far, whole):
    half = near.shape[0]
    whole[:half] = near[...]
    whole[half:] = far[...]


def pair_step(width, count, mine, theirs, *rest):
    *held, out = rest
    for source, copy in zip(held[: len(held) // 2], held[len(held) // 2 :]):
        copy[...] = source[...]
    out[...] = (mine[...] + theirs[...].astype(F32)).astype(BF16)
    if count:
        tail = tail_of(width)
        tile = mine[:, tail] + theirs[:, tail].astype(F32)
        out[:, tail] = with_stats(tile, width, read_stats(tile, width, count)).astype(BF16)


def swap(values):
    return lax.ppermute(values, "core", [(0, 1), (1, 0)])


def gathered(copies):
    near = flat(exchange(copies, "rows"))
    return near, swap(near)


def reduced(mine, theirs, width, count, *held):
    *held, message = local(
        lambda *refs: pair_step(width, count, *refs),
        [*((x.shape, x.dtype) for x in held), (mine.shape, BF16)],
        mine,
        swap(theirs),
        *held,
    )
    return (exchange(message, "rows"), *held)


def gate_step(
    near, far, gains, gate_weight, up_weight, target_rows, ids, weights, out, inputs, *kept
):
    rejoin(near, far, inputs)
    for source, copy in zip((target_rows, ids, weights, gains), kept):
        copy[...] = source[...]
    width = gate_weight.shape[1]
    values = inputs[...].astype(F32)
    scaled = (values * gains[0:1]).astype(BF16)
    squares = jnp.sum(values * values, axis=1, keepdims=True)
    put(out, contract(scaled, gate_weight[...], 1, 0).astype(BF16), [squares])
    out[:, padded(width) : padded(width) + width] = contract(
        scaled, up_weight[...], 1, 0
    ).astype(BF16)


def active_step(model, width, message, gate, upward, gelu_gate, gelu_slope, out):
    (squares,) = read_stats(summed(message, tail_of(width)), width, 1)
    scale = lax.rsqrt(squares / model + EPS)
    gate_value = summed(message, slice(0, width)) * scale
    up_value = summed(message, slice(padded(width), padded(width) + width)) * scale
    value, slope = gelu_parts(gate_value)
    gate[...] = gate_value
    upward[...] = up_value
    gelu_gate[...] = value
    gelu_slope[...] = slope
    put_copies(out, (value * up_value).astype(BF16), [squares])


def branch_step(message, down_weight, target_rows, mine, theirs):
    hidden, width = down_weight.shape
    half = mine.shape[0]
    block = contract(message[:, :hidden], down_weight[...], 1, 0)
    mine[:, :width] = block[:half]
    theirs[:, :width] = block[half:].astype(BF16)
    mine[:, width : 2 * width] = target_rows[:half].astype(F32)
    theirs[:, width : 2 * width] = target_rows[half:]


def norm_step(message, inputs, gains, head, branch, target, out):
    del head
    width = branch.shape[1]
    both = summed(message, slice(0, 2 * width))
    value = both[:, :width]
    branch[...] = value
    target[...] = both[:, width:]
    bent = value * gains[1:2]
    own = inputs[...].astype(F32)
    stats = [
        jnp.sum(x, axis=1, keepdims=True) for x in (value * value, own * bent, bent * bent, own * own)
    ]
    lane = lax.broadcasted_iota(jnp.int32, out.shape[1:], 1)
    tile = jnp.zeros(out.shape[1:], F32)
    for i, stat in enumerate(stats):
        tile = jnp.where(lane == i, stat, tile)
    for i in range(out.shape[0]):
        out[i] = tile


def scale_step(model, message, branch, scales, out):
    tile = message[0]
    for i in range(1, message.shape[0]):
        tile = tile + message[i]
    lane = lax.broadcasted_iota(jnp.int32, tile.shape, 1)
    square, cross, bent, own = [
        jnp.sum(jnp.where(lane == i, tile, 0.0), axis=1, keepdims=True) for i in range(4)
    ]
    post = lax.rsqrt(square / model + EPS)
    final_squares = own + post * (2.0 * cross + post * bent)
    final = lax.rsqrt(jnp.maximum(final_squares, 0.0) / model + EPS)
    pre = lax.rsqrt(own / model + EPS)
    scales[...] = jnp.where(lane == 0, post, jnp.where(lane == 1, final, pre))
    put_copies(out, branch[...].astype(BF16), [post, final])


def logit_step(near, far, inputs, gains, head, out, final_out, message, final, sem):
    rejoin(near, far, message)
    width = final.shape[1]
    post, scale = read_stats(message[:, tail_of(width)].astype(F32), width, 2)
    resid = inputs[...].astype(F32) + message[:, :width].astype(F32) * post * gains[1:2]
    final[...] = (resid * scale * gains[2:3]).astype(BF16)
    copy = pltpu.make_async_copy(final, final_out, sem)
    copy.start()
    for i in range(0, head.shape[1], CHUNK):
        columns = slice(i, i + CHUNK)
        out[:, columns] = contract(final[...], head[:, columns], 1, 0).astype(BF16)
    copy.wait()


def soft_step(message, ids, out):
    rows, vocab = message.shape[1:]
    step = 256
    others = jnp.zeros((rows, step), F32)
    cross = jnp.zeros((rows, step), F32)
    target = jnp.zeros((rows, step), F32)
    lane = lax.broadcasted_iota(jnp.int32, (rows, step), 1)
    for i in range(vocab // step):
        columns = slice(i * step, (i + 1) * step)
        logits = summed(message, columns)
        hits = lane == ids[...] - i * step
        bent = jnp.tanh(logits / CAP)
        raised = jnp.where(hits, 0.0, jnp.exp(CAP * bent - CAP))
        sloped = raised * (1.0 - bent * bent)
        others = others + raised
        cross = cross + sloped * logits
        target = target + jnp.where(hits, logits, 0.0)
        part = sloped.astype(BF16)
        for j in range(out.shape[0]):
            out[j, :, columns] = part
    stats = [jnp.sum(x, axis=1, keepdims=True) for x in (others, cross, target)]
    tile = with_stats(jnp.zeros((rows, LANES), F32), vocab, stats).astype(BF16)
    for j in range(out.shape[0]):
        out[j, :, vocab : vocab + LANES] = tile


def row_step(message, head, mine, theirs):
    vocab = head.shape[1]
    total = contract(message[:, :vocab], head[...], 1, 1)
    stats = read_stats(message[:, vocab : vocab + LANES].astype(F32), vocab, 3)
    put_halves(mine, theirs, total, stats)


def resid_step(
    model, message, target_rows, branch, inputs, scales, weights, gains, grad_resid, out
):
    width = branch.shape[1]
    others, cross, logit = read_stats(summed(message, tail_of(width)), width, 3)
    bent = jnp.tanh(logit / CAP)
    target = CAP * bent
    total = others + jnp.exp(target - CAP)
    logprob = target - CAP - jnp.log(total)
    spread = weights[...] / total
    pull = -spread * others * (1.0 - bent * bent)
    post = scales[:, 0:1]
    final = scales[:, 1:2]
    post_gain = gains[1:2]
    final_gain = gains[2:3]
    grad_final = spread * summed(message, slice(0, width)) + pull * target_rows[...]
    back_final = (spread * cross + pull * logit) / final
    value = branch[...]
    resid = inputs[...].astype(F32) + post * value * post_gain
    grad = final * grad_final * final_gain - resid * (
        final * final * final * back_final / model
    )
    grad_resid[...] = grad
    weighted = grad * post_gain
    back_post = jnp.sum(weighted * value, axis=1, keepdims=True)
    put_copies(
        out,
        (post * weighted).astype(BF16),
        [spread, pull, weights[...] * logprob, back_post],
    )


def down_step(copies_n, near, far, branch, down_weight, out, message, loss):
    rejoin(near, far, message)
    hidden, width = down_weight.shape
    tail = tail_of(width)
    _, _, score, back_post = read_stats(message[:, tail].astype(F32), width, 4)
    post, _ = read_stats(branch[:, tail].astype(F32), width, 2)
    put(
        out,
        contract(message[:, :width], down_weight[...], 1, 1).astype(BF16),
        [back_post, post / copies_n],
    )
    out[:, padded(hidden) : padded(hidden) + hidden] = contract(
        branch[:, :width], down_weight[...], 1, 1
    ).astype(BF16)
    loss[...] = -jnp.sum(score, axis=0, keepdims=True) / message.shape[0]


def hidden_step(model, message, gate, upward, gelu_gate, gelu_slope, out):
    width = gate.shape[1]
    start = padded(width)
    back_post, post = read_stats(summed(message, tail_of(width)), width, 2)
    grad = summed(message, slice(0, width)) - summed(message, slice(start, start + width)) * (
        post * post * post * back_post / model
    )
    gate_in = (grad * upward[...] * gelu_slope[...]).astype(BF16)
    up_in = (grad * gelu_gate[...]).astype(BF16)
    back = jnp.sum(
        gate_in.astype(F32) * gate[...] + up_in.astype(F32) * upward[...], axis=1, keepdims=True
    )
    put(out.at[0], gate_in, [back, back_post])
    out[0, :, start : start + width] = up_in
    whole = out[0]
    for i in range(1, out.shape[0]):
        out[i] = whole


def normed_step(
    model, message, gate_weight, up_weight, active, branch, weighted, mine, theirs, rates
):
    width, hidden = gate_weight.shape
    start = padded(hidden)
    total = contract(message[:, :hidden], gate_weight[...], 1, 1) + contract(
        message[:, start : start + hidden], up_weight[...], 1, 1
    )
    back, back_post = read_stats(message[:, tail_of(hidden)].astype(F32), hidden, 2)
    put_halves(mine, theirs, total, [back])
    (squares,) = read_stats(active[:, tail_of(hidden)].astype(F32), hidden, 1)
    (post,) = read_stats(branch[:, tail_of(width)].astype(F32), width, 1)
    spread, pull = read_stats(weighted[:, tail_of(width)].astype(F32), width, 2)
    lane = lax.broadcasted_iota(jnp.int32, rates.shape, 1)
    tile = jnp.where(lane == 0, spread, pull)
    tile = jnp.where(lane == 2, post * post * post * back_post / model, tile)
    rates[...] = jnp.where(lane == 3, lax.rsqrt(squares / model + EPS), tile)


def last_step(model, message, grad_resid, inputs, scales, gains, out):
    width = out.shape[1]
    scale = scales[:, 2:3]
    (back,) = read_stats(summed(message, tail_of(width)), width, 1)
    weighted = summed(message, slice(0, width)) * gains[0:1]
    out[...] = (
        grad_resid[...] + scale * weighted - inputs[...].astype(F32) * (scale * scale * back / model)
    ).astype(BF16)


def shards(
    hidden,
    pre_gain,
    post_gain,
    final_gain,
    gate_weight,
    up_weight,
    down_weight,
    head_weight,
    token_ids,
    rewards,
):
    tok_dev, width = hidden.shape
    tokens = token_ids.shape[0]
    rows_n = lax.axis_size("rows")
    cols_n = lax.axis_size("width")
    model = width * cols_n
    ff = gate_weight.shape[1]
    vocab = head_weight.shape[1]
    sub = tokens // cols_n
    half = tokens // 2
    core = lax.axis_index("core")
    vocab_index = lax.axis_index("rows") * 2 + core
    width_index = lax.axis_index("width")
    gains = jnp.stack([pre_gain, post_gain, final_gain])

    weights = jnp.repeat(rewards, tokens // rewards.shape[0])
    own_weights = lax.dynamic_slice_in_dim(weights, vocab_index * tok_dev, tok_dev, 0)[:, None]
    ids = token_ids.reshape(rows_n, 2, tok_dev)
    ids = jnp.where(core == 0, jnp.swapaxes(ids, 0, 1), jnp.swapaxes(ids[:, ::-1], 0, 1))
    ids = ids.reshape(tokens) - vocab_index * vocab
    hits = jnp.arange(vocab, dtype=jnp.int32)[None, :] == ids[:, None]
    sub_ids = lax.dynamic_slice_in_dim(ids, width_index * sub, sub, 0)[:, None]
    target_part = contract(hits.astype(BF16), head_weight, 1, 1).astype(BF16)
    near, far = gathered(jnp.broadcast_to(hidden[None], (rows_n, tok_dev, width)))
    message, inputs, target_part, sub_ids, own_weights, gains = local(
        gate_step,
        [
            ((tokens, padded(ff) * 2), BF16),
            ((tokens, width), BF16),
            ((tokens, width), BF16),
            ((sub, 1), jnp.int32),
            ((tok_dev, 1), F32),
            ((3, width), F32),
        ],
        near,
        far,
        gains,
        gate_weight,
        up_weight,
        target_part,
        sub_ids,
        own_weights,
    )
    gate, upward, gelu_gate, gelu_slope, message = local(
        lambda *refs: active_step(model, ff, *refs),
        [((sub, ff), F32)] * 4 + [((cols_n, sub, padded(ff)), BF16)],
        exchange(message, "width"),
    )
    active = flat(exchange(message, "width"))
    mine, theirs = local(
        branch_step,
        [((half, width * 2), F32), ((half, width * 2), BF16)],
        active,
        down_weight,
        target_part,
    )
    branch, target_rows, message = local(
        norm_step,
        [((tok_dev, width), F32)] * 2 + [((cols_n, tok_dev, LANES), F32)],
        *reduced(mine, theirs, width * 2, 0),
        hidden,
        gains,
        head_weight,
    )
    scales, message = local(
        lambda *refs: scale_step(model, *refs),
        [((tok_dev, LANES), F32), ((rows_n, tok_dev, padded(width)), BF16)],
        exchange(message, "width"),
        branch,
    )
    near, far = gathered(message)
    message, final, branch_all = local(
        logit_step,
        [
            ((tokens, vocab), BF16),
            ((tokens, width), BF16),
            ((tokens, padded(width)), BF16),
        ],
        near,
        far,
        inputs,
        gains,
        head_weight,
        off_chip=(1,),
        scratch=(pltpu.VMEM((tokens, width), BF16), pltpu.SemaphoreType.DMA),
    )
    (message,) = local(
        soft_step,
        [((cols_n, sub, vocab + LANES), BF16)],
        exchange(message, "width"),
        sub_ids,
    )
    sloped = flat(exchange(message, "width"))
    halves = [((half, padded(width)), F32), ((half, padded(width)), BF16)]
    mine, theirs = local(row_step, halves, sloped, head_weight)
    grad_resid, message = local(
        lambda *refs: resid_step(model, *refs),
        [((tok_dev, width), F32), ((rows_n, tok_dev, padded(width)), BF16)],
        *reduced(mine, theirs, width, 3),
        target_rows,
        branch,
        hidden,
        scales,
        own_weights,
        gains,
    )
    near, far = gathered(message)
    message, weighted, loss = local(
        lambda *refs: down_step(cols_n, *refs),
        [((tokens, padded(ff) * 2), BF16), ((tokens, padded(width)), BF16), ((1, 1), F32)],
        near,
        far,
        branch_all,
        down_weight,
    )
    (message,) = local(
        lambda *refs: hidden_step(model, *refs),
        [((cols_n, sub, padded(ff) * 2), BF16)],
        exchange(message, "width"),
        gate,
        upward,
        gelu_gate,
        gelu_slope,
    )
    grads_in = flat(exchange(message, "width"))
    mine, theirs, rates = local(
        lambda *refs: normed_step(model, *refs),
        [*halves, ((tokens, LANES), F32)],
        grads_in,
        gate_weight,
        up_weight,
        active,
        branch_all,
        weighted,
    )
    message, rates = reduced(mine, theirs, width, 1, rates)
    (grad_hidden,) = local(
        lambda *refs: last_step(model, *refs),
        [((tok_dev, width), BF16)],
        message,
        grad_resid,
        hidden,
        scales,
        gains,
    )

    spread, pull, along, scale_pre = [rates[:, i : i + 1] for i in range(4)]
    delta = (spread * sloped[:, :vocab].astype(F32) + jnp.where(hits, pull, 0.0)).astype(BF16)
    grad_head = contract(final, delta, 0, 0).astype(BF16)
    grad_branch = (
        weighted[:, :width].astype(F32) - branch_all[:, :width].astype(F32) * along
    ).astype(BF16)
    grad_down = contract(active[:, :ff], grad_branch, 0, 0).astype(BF16)
    normed = (inputs.astype(F32) * scale_pre * pre_gain).astype(BF16)
    grad_gate = contract(normed, grads_in[:, :ff], 0, 0).astype(BF16)
    grad_up = contract(normed, grads_in[:, padded(ff) : padded(ff) + ff], 0, 0).astype(BF16)
    return (grad_hidden, grad_gate, grad_up, grad_down, grad_head, loss[0, 0])


def solution(mesh):
    devices = mesh.devices
    vocab = ("rows", "core")
    return jax.shard_map(
        shards,
        mesh=Mesh(
            devices.reshape(devices.shape[0] // 2, 2, devices.shape[1]), (*vocab, "width")
        ),
        in_specs=(
            P(vocab, "width"),
            P("width"),
            P("width"),
            P("width"),
            P("width", vocab),
            P("width", vocab),
            P(vocab, "width"),
            P("width", vocab),
            P(),
            P(),
        ),
        out_specs=(
            P(vocab, "width"),
            P("width", vocab),
            P("width", vocab),
            P(vocab, "width"),
            P("width", vocab),
            P(),
        ),
        check_vma=False,
    )
```

```python
import math

import jax
import jax.numpy as jnp
from jax import lax
from jax.experimental import pallas as pl
from jax.experimental.pallas import tpu as pltpu
from jax.sharding import Mesh
from jax.sharding import PartitionSpec as P

CAP = 30.0
EPS = 1e-06
ROOT_TWO_PI = math.sqrt(2.0 / math.pi)
BF16 = jnp.bfloat16
F32 = jnp.float32
LANES = 128
CHUNK = 512


def contract(left, right, left_dim, right_dim):
    return lax.dot_general(
        left, right, (((left_dim,), (right_dim,)), ((), ())), preferred_element_type=F32
    )


def gelu_parts(value):
    square = value * value
    bent = jnp.tanh(ROOT_TWO_PI * value * (1.0 + 0.044715 * square))
    half = 0.5 * (1.0 + bent)
    slope = half + 0.5 * value * (1.0 - bent * bent) * ROOT_TWO_PI * (1.0 + 3.0 * 0.044715 * square)
    return value * half, slope


def padded(width):
    return width // LANES * LANES + LANES


def pick(tile, at):
    lane = lax.broadcasted_iota(jnp.int32, tile.shape, 1)
    return jnp.sum(jnp.where((lane == at) | (lane == at + 1), tile, 0.0), axis=1, keepdims=True)


def read_stats(tile, width, count):
    return [pick(tile, width % LANES + 2 * i) for i in range(count)]


def tail_of(width):
    return slice(width // LANES * LANES, padded(width))


def with_stats(tile, width, stats):
    lane = lax.broadcasted_iota(jnp.int32, tile.shape, 1)
    at = width % LANES
    tile = jnp.where(lane < at, tile, 0.0)
    for i, stat in enumerate(stats):
        high = stat.astype(BF16).astype(F32)
        tile = jnp.where(lane == at + 2 * i, high, tile)
        tile = jnp.where(lane == at + 2 * i + 1, stat - high, tile)
    return tile


def put(ref, block, stats):
    width = block.shape[1]
    ref[:, :width] = block
    tail = tail_of(width)
    ref[:, tail] = with_stats(ref[:, tail].astype(F32), width, stats).astype(ref.dtype)


def put_halves(mine, theirs, block, stats):
    half = mine.shape[0]
    put(mine, block[:half], [stat[:half] for stat in stats])
    put(theirs, block[half:].astype(BF16), [stat[half:] for stat in stats])


def put_copies(ref, block, stats):
    put(ref.at[0], block, stats)
    whole = ref[0]
    for i in range(1, ref.shape[0]):
        ref[i] = whole


def summed(ref, columns):
    total = ref[0, :, columns].astype(F32)
    for i in range(1, ref.shape[0]):
        total = total + ref[i, :, columns].astype(F32)
    return total


def local(body, outs, *args):
    return pl.pallas_call(
        body,
        out_shape=tuple(jax.ShapeDtypeStruct(s, d) for s, d in outs),
        in_specs=[pl.BlockSpec(memory_space=pltpu.VMEM) for _ in args],
        out_specs=tuple(pl.BlockSpec(memory_space=pltpu.VMEM) for _ in outs),
        compiler_params=pltpu.CompilerParams(vmem_limit_bytes=16 << 20),
    )(*args)


def exchange(parts, axis):
    size = lax.axis_size(axis)
    if parts.ndim == 2:
        parts = parts.reshape(size, parts.shape[0] // size, parts.shape[1])
    return lax.all_to_all(parts, axis, 0, 0, tiled=True)


def flat(message):
    return message.reshape(message.shape[0] * message.shape[1], message.shape[2])


def rejoin(near, far, whole):
    half = near.shape[0]
    whole[:half] = near[...]
    whole[half:] = far[...]


def pair_step(width, count, mine, theirs, *rest):
    *held, out = rest
    for source, copy in zip(held[: len(held) // 2], held[len(held) // 2 :]):
        copy[...] = source[...]
    out[...] = (mine[...] + theirs[...].astype(F32)).astype(BF16)
    if count:
        tail = tail_of(width)
        tile = mine[:, tail] + theirs[:, tail].astype(F32)
        out[:, tail] = with_stats(tile, width, read_stats(tile, width, count)).astype(BF16)


def swap(values):
    return lax.ppermute(values, "core", [(0, 1), (1, 0)])


def gathered(copies):
    near = flat(exchange(copies, "rows"))
    return near, swap(near)


def reduced(mine, theirs, width, count, *held):
    *held, message = local(
        lambda *refs: pair_step(width, count, *refs),
        [*((x.shape, x.dtype) for x in held), (mine.shape, BF16)],
        mine,
        swap(theirs),
        *held,
    )
    return (exchange(message, "rows"), *held)


def gate_step(
    near, far, gains, gate_weight, up_weight, target_rows, ids, weights, out, inputs, *kept
):
    rejoin(near, far, inputs)
    for source, copy in zip((target_rows, ids, weights, gains), kept):
        copy[...] = source[...]
    width = gate_weight.shape[1]
    values = inputs[...].astype(F32)
    scaled = (values * gains[0:1]).astype(BF16)
    squares = jnp.sum(values * values, axis=1, keepdims=True)
    put(out, contract(scaled, gate_weight[...], 1, 0).astype(BF16), [squares])
    out[:, padded(width) : padded(width) + width] = contract(
        scaled, up_weight[...], 1, 0
    ).astype(BF16)


def active_step(model, width, message, gate, upward, gelu_gate, gelu_slope, out):
    (squares,) = read_stats(summed(message, tail_of(width)), width, 1)
    scale = lax.rsqrt(squares / model + EPS)
    gate_value = summed(message, slice(0, width)) * scale
    up_value = summed(message, slice(padded(width), padded(width) + width)) * scale
    value, slope = gelu_parts(gate_value)
    gate[...] = gate_value
    upward[...] = up_value
    gelu_gate[...] = value
    gelu_slope[...] = slope
    put_copies(out, (value * up_value).astype(BF16), [squares])


def branch_step(message, down_weight, target_rows, mine, theirs):
    hidden, width = down_weight.shape
    half = mine.shape[0]
    block = contract(message[:, :hidden], down_weight[...], 1, 0)
    mine[:, :width] = block[:half]
    theirs[:, :width] = block[half:].astype(BF16)
    mine[:, width : 2 * width] = target_rows[:half].astype(F32)
    theirs[:, width : 2 * width] = target_rows[half:]


def norm_step(message, inputs, gains, head, branch, target, out):
    del head
    width = branch.shape[1]
    both = summed(message, slice(0, 2 * width))
    value = both[:, :width]
    branch[...] = value
    target[...] = both[:, width:]
    bent = value * gains[1:2]
    own = inputs[...].astype(F32)
    stats = [
        jnp.sum(x, axis=1, keepdims=True) for x in (value * value, own * bent, bent * bent, own * own)
    ]
    lane = lax.broadcasted_iota(jnp.int32, out.shape[1:], 1)
    tile = jnp.zeros(out.shape[1:], F32)
    for i, stat in enumerate(stats):
        tile = jnp.where(lane == i, stat, tile)
    for i in range(out.shape[0]):
        out[i] = tile


def scale_step(model, message, branch, scales, out):
    tile = message[0]
    for i in range(1, message.shape[0]):
        tile = tile + message[i]
    lane = lax.broadcasted_iota(jnp.int32, tile.shape, 1)
    square, cross, bent, own = [
        jnp.sum(jnp.where(lane == i, tile, 0.0), axis=1, keepdims=True) for i in range(4)
    ]
    post = lax.rsqrt(square / model + EPS)
    final_squares = own + post * (2.0 * cross + post * bent)
    final = lax.rsqrt(jnp.maximum(final_squares, 0.0) / model + EPS)
    scales[...] = jnp.where(lane == 0, post, final)
    put_copies(out, branch[...].astype(BF16), [post, final])


def logit_step(near, far, inputs, gains, head, out, final, message):
    rejoin(near, far, message)
    width = final.shape[1]
    post, scale = read_stats(message[:, tail_of(width)].astype(F32), width, 2)
    resid = inputs[...].astype(F32) + message[:, :width].astype(F32) * post * gains[1:2]
    final[...] = (resid * scale * gains[2:3]).astype(BF16)
    for i in range(0, head.shape[1], CHUNK):
        columns = slice(i, i + CHUNK)
        out[:, columns] = contract(final[...], head[:, columns], 1, 0).astype(BF16)


def soft_step(message, ids, out):
    rows, vocab = message.shape[1:]
    step = 256
    others = jnp.zeros((rows, step), F32)
    cross = jnp.zeros((rows, step), F32)
    target = jnp.zeros((rows, step), F32)
    lane = lax.broadcasted_iota(jnp.int32, (rows, step), 1)
    for i in range(vocab // step):
        columns = slice(i * step, (i + 1) * step)
        logits = summed(message, columns)
        hits = lane == ids[...] - i * step
        bent = jnp.tanh(logits / CAP)
        raised = jnp.where(hits, 0.0, jnp.exp(CAP * bent - CAP))
        sloped = raised * (1.0 - bent * bent)
        others = others + raised
        cross = cross + sloped * logits
        target = target + jnp.where(hits, logits, 0.0)
        part = sloped.astype(BF16)
        for j in range(out.shape[0]):
            out[j, :, columns] = part
    stats = [jnp.sum(x, axis=1, keepdims=True) for x in (others, cross, target)]
    tile = with_stats(jnp.zeros((rows, LANES), F32), vocab, stats).astype(BF16)
    for j in range(out.shape[0]):
        out[j, :, vocab : vocab + LANES] = tile


def row_step(message, head, mine, theirs):
    vocab = head.shape[1]
    total = contract(message[:, :vocab], head[...], 1, 1)
    stats = read_stats(message[:, vocab : vocab + LANES].astype(F32), vocab, 3)
    put_halves(mine, theirs, total, stats)


def resid_step(
    model, message, target_rows, branch, inputs, scales, weights, gains, grad_resid, out
):
    width = branch.shape[1]
    others, cross, logit = read_stats(summed(message, tail_of(width)), width, 3)
    bent = jnp.tanh(logit / CAP)
    target = CAP * bent
    total = others + jnp.exp(target - CAP)
    logprob = target - CAP - jnp.log(total)
    spread = weights[...] / total
    pull = -spread * others * (1.0 - bent * bent)
    post = scales[:, 0:1]
    final = scales[:, 1:2]
    post_gain = gains[1:2]
    final_gain = gains[2:3]
    grad_final = spread * summed(message, slice(0, width)) + pull * target_rows[...]
    back_final = (spread * cross + pull * logit) / final
    value = branch[...]
    resid = inputs[...].astype(F32) + post * value * post_gain
    grad = final * grad_final * final_gain - resid * (
        final * final * final * back_final / model
    )
    grad_resid[...] = grad
    weighted = grad * post_gain
    back_post = jnp.sum(weighted * value, axis=1, keepdims=True)
    put_copies(
        out,
        (post * weighted).astype(BF16),
        [spread, pull, weights[...] * logprob, back_post],
    )


def down_step(copies_n, near, far, branch, down_weight, out, message, loss):
    rejoin(near, far, message)
    hidden, width = down_weight.shape
    tail = tail_of(width)
    _, _, score, back_post = read_stats(message[:, tail].astype(F32), width, 4)
    post, _ = read_stats(branch[:, tail].astype(F32), width, 2)
    put(
        out,
        contract(message[:, :width], down_weight[...], 1, 1).astype(BF16),
        [back_post, post / copies_n],
    )
    out[:, padded(hidden) : padded(hidden) + hidden] = contract(
        branch[:, :width], down_weight[...], 1, 1
    ).astype(BF16)
    loss[...] = -jnp.sum(score, axis=0, keepdims=True) / message.shape[0]


def hidden_step(model, message, gate, upward, gelu_gate, gelu_slope, out):
    width = gate.shape[1]
    start = padded(width)
    back_post, post = read_stats(summed(message, tail_of(width)), width, 2)
    grad = summed(message, slice(0, width)) - summed(message, slice(start, start + width)) * (
        post * post * post * back_post / model
    )
    gate_in = (grad * upward[...] * gelu_slope[...]).astype(BF16)
    up_in = (grad * gelu_gate[...]).astype(BF16)
    back = jnp.sum(
        gate_in.astype(F32) * gate[...] + up_in.astype(F32) * upward[...], axis=1, keepdims=True
    )
    put(out.at[0], gate_in, [back, back_post])
    out[0, :, start : start + width] = up_in
    whole = out[0]
    for i in range(1, out.shape[0]):
        out[i] = whole


def normed_step(
    model,
    message,
    gate_weight,
    up_weight,
    active,
    branch,
    weighted,
    gains,
    final,
    mine,
    theirs,
    rates,
    final_copy,
):
    final_copy[...] = final[...]
    width, hidden = gate_weight.shape
    start = padded(hidden)
    total = contract(message[:, :hidden], gate_weight[...], 1, 1) + contract(
        message[:, start : start + hidden], up_weight[...], 1, 1
    )
    back, back_post = read_stats(message[:, tail_of(hidden)].astype(F32), hidden, 2)
    (squares,) = read_stats(active[:, tail_of(hidden)].astype(F32), hidden, 1)
    scale = lax.rsqrt(squares / model + EPS)
    put_halves(mine, theirs, total * scale * gains[0:1], [scale * scale * back / model])
    (post,) = read_stats(branch[:, tail_of(width)].astype(F32), width, 1)
    spread, pull = read_stats(weighted[:, tail_of(width)].astype(F32), width, 2)
    lane = lax.broadcasted_iota(jnp.int32, rates.shape, 1)
    tile = jnp.where(lane == 0, spread, pull)
    tile = jnp.where(lane == 2, post * post * post * back_post / model, tile)
    rates[...] = jnp.where(lane == 3, scale, tile)


def last_step(message, grad_resid, inputs, out):
    width = out.shape[1]
    (back,) = read_stats(summed(message, tail_of(width)), width, 1)
    total = grad_resid[...] + summed(message, slice(0, width))
    out[...] = (total - inputs[...].astype(F32) * back).astype(BF16)


def shards(
    hidden,
    pre_gain,
    post_gain,
    final_gain,
    gate_weight,
    up_weight,
    down_weight,
    head_weight,
    token_ids,
    rewards,
):
    tok_dev, width = hidden.shape
    tokens = token_ids.shape[0]
    rows_n = lax.axis_size("rows")
    cols_n = lax.axis_size("width")
    model = width * cols_n
    ff = gate_weight.shape[1]
    vocab = head_weight.shape[1]
    sub = tokens // cols_n
    half = tokens // 2
    core = lax.axis_index("core")
    vocab_index = lax.axis_index("rows") * 2 + core
    width_index = lax.axis_index("width")
    gains = jnp.stack([pre_gain, post_gain, final_gain])

    weights = jnp.repeat(rewards, tokens // rewards.shape[0])
    own_weights = lax.dynamic_slice_in_dim(weights, vocab_index * tok_dev, tok_dev, 0)[:, None]
    ids = token_ids.reshape(rows_n, 2, tok_dev)
    ids = jnp.where(core == 0, jnp.swapaxes(ids, 0, 1), jnp.swapaxes(ids[:, ::-1], 0, 1))
    ids = ids.reshape(tokens) - vocab_index * vocab
    hits = jnp.arange(vocab, dtype=jnp.int32)[None, :] == ids[:, None]
    sub_ids = lax.dynamic_slice_in_dim(ids, width_index * sub, sub, 0)[:, None]
    target_part = contract(hits.astype(BF16), head_weight, 1, 1).astype(BF16)
    near, far = gathered(jnp.broadcast_to(hidden[None], (rows_n, tok_dev, width)))
    message, inputs, target_part, sub_ids, own_weights, gains = local(
        gate_step,
        [
            ((tokens, padded(ff) * 2), BF16),
            ((tokens, width), BF16),
            ((tokens, width), BF16),
            ((sub, 1), jnp.int32),
            ((tok_dev, 1), F32),
            ((3, width), F32),
        ],
        near,
        far,
        gains,
        gate_weight,
        up_weight,
        target_part,
        sub_ids,
        own_weights,
    )
    gate, upward, gelu_gate, gelu_slope, message = local(
        lambda *refs: active_step(model, ff, *refs),
        [((sub, ff), F32)] * 4 + [((cols_n, sub, padded(ff)), BF16)],
        exchange(message, "width"),
    )
    active = flat(exchange(message, "width"))
    mine, theirs = local(
        branch_step,
        [((half, width * 2), F32), ((half, width * 2), BF16)],
        active,
        down_weight,
        target_part,
    )
    branch, target_rows, message = local(
        norm_step,
        [((tok_dev, width), F32)] * 2 + [((cols_n, tok_dev, LANES), F32)],
        *reduced(mine, theirs, width * 2, 0),
        hidden,
        gains,
        head_weight,
    )
    scales, message = local(
        lambda *refs: scale_step(model, *refs),
        [((tok_dev, LANES), F32), ((rows_n, tok_dev, padded(width)), BF16)],
        exchange(message, "width"),
        branch,
    )
    near, far = gathered(message)
    message, final, branch_all = local(
        logit_step,
        [
            ((tokens, vocab), BF16),
            ((tokens, width), BF16),
            ((tokens, padded(width)), BF16),
        ],
        near,
        far,
        inputs,
        gains,
        head_weight,
    )
    (message,) = local(
        soft_step,
        [((cols_n, sub, vocab + LANES), BF16)],
        exchange(message, "width"),
        sub_ids,
    )
    sloped = flat(exchange(message, "width"))
    halves = [((half, padded(width)), F32), ((half, padded(width)), BF16)]
    mine, theirs = local(row_step, halves, sloped, head_weight)
    grad_resid, message = local(
        lambda *refs: resid_step(model, *refs),
        [((tok_dev, width), F32), ((rows_n, tok_dev, padded(width)), BF16)],
        *reduced(mine, theirs, width, 3),
        target_rows,
        branch,
        hidden,
        scales,
        own_weights,
        gains,
    )
    near, far = gathered(message)
    message, weighted, loss = local(
        lambda *refs: down_step(cols_n, *refs),
        [((tokens, padded(ff) * 2), BF16), ((tokens, padded(width)), BF16), ((1, 1), F32)],
        near,
        far,
        branch_all,
        down_weight,
    )
    (message,) = local(
        lambda *refs: hidden_step(model, *refs),
        [((cols_n, sub, padded(ff) * 2), BF16)],
        exchange(message, "width"),
        gate,
        upward,
        gelu_gate,
        gelu_slope,
    )
    grads_in = flat(exchange(message, "width"))
    mine, theirs, rates, final = local(
        lambda *refs: normed_step(model, *refs),
        [*halves, ((tokens, LANES), F32), ((tokens, width), BF16)],
        grads_in,
        gate_weight,
        up_weight,
        active,
        branch_all,
        weighted,
        gains,
        final,
    )
    scale_pre = rates[:, 3:4]
    message, rates = reduced(mine, theirs, width, 1, rates)
    (grad_hidden,) = local(
        last_step,
        [((tok_dev, width), BF16)],
        message,
        grad_resid,
        hidden,
    )

    spread, pull, along, late_scale = [rates[:, i : i + 1] for i in range(4)]
    delta = (spread * sloped[:, :vocab].astype(F32) + jnp.where(hits, pull, 0.0)).astype(BF16)
    grad_head = contract(final, delta, 0, 0).astype(BF16)
    grad_branch = (
        weighted[:, :width].astype(F32) - branch_all[:, :width].astype(F32) * along
    ).astype(BF16)
    grad_down = contract(active[:, :ff], grad_branch, 0, 0).astype(BF16)
    normed = (inputs.astype(F32) * scale_pre * pre_gain).astype(BF16)
    grad_gate = contract(normed, grads_in[:, :ff], 0, 0).astype(BF16)
    normed = (inputs.astype(F32) * late_scale * pre_gain).astype(BF16)
    grad_up = contract(normed, grads_in[:, padded(ff) : padded(ff) + ff], 0, 0).astype(BF16)
    return (grad_hidden, grad_gate, grad_up, grad_down, grad_head, loss[0, 0])


def solution(mesh):
    devices = mesh.devices
    vocab = ("rows", "core")
    return jax.shard_map(
        shards,
        mesh=Mesh(
            devices.reshape(devices.shape[0] // 2, 2, devices.shape[1]), (*vocab, "width")
        ),
        in_specs=(
            P(vocab, "width"),
            P("width"),
            P("width"),
            P("width"),
            P("width", vocab),
            P("width", vocab),
            P(vocab, "width"),
            P("width", vocab),
            P(),
            P(),
        ),
        out_specs=(
            P(vocab, "width"),
            P("width", vocab),
            P("width", vocab),
            P(vocab, "width"),
            P("width", vocab),
            P(),
        ),
        check_vma=False,
    )
```

```python
import math

import jax
import jax.numpy as jnp
from jax import lax
from jax.experimental import pallas as pl
from jax.experimental.pallas import tpu as pltpu
from jax.sharding import Mesh
from jax.sharding import PartitionSpec as P

CAP = 30.0
EPS = 1e-06
ROOT_TWO_PI = math.sqrt(2.0 / math.pi)
BF16 = jnp.bfloat16
F32 = jnp.float32
LANES = 128
CHUNK = 512


def contract(left, right, left_dim, right_dim):
    return lax.dot_general(
        left, right, (((left_dim,), (right_dim,)), ((), ())), preferred_element_type=F32
    )


def gelu_parts(value):
    square = value * value
    bent = jnp.tanh(ROOT_TWO_PI * value * (1.0 + 0.044715 * square))
    half = 0.5 * (1.0 + bent)
    slope = half + 0.5 * value * (1.0 - bent * bent) * ROOT_TWO_PI * (1.0 + 3.0 * 0.044715 * square)
    return value * half, slope


def padded(width):
    return width // LANES * LANES + LANES


def pick(tile, at):
    lane = lax.broadcasted_iota(jnp.int32, tile.shape, 1)
    return jnp.sum(jnp.where((lane == at) | (lane == at + 1), tile, 0.0), axis=1, keepdims=True)


def read_stats(tile, width, count):
    return [pick(tile, width % LANES + 2 * i) for i in range(count)]


def tail_of(width):
    return slice(width // LANES * LANES, padded(width))


def with_stats(tile, width, stats):
    lane = lax.broadcasted_iota(jnp.int32, tile.shape, 1)
    at = width % LANES
    tile = jnp.where(lane < at, tile, 0.0)
    for i, stat in enumerate(stats):
        high = stat.astype(BF16).astype(F32)
        tile = jnp.where(lane == at + 2 * i, high, tile)
        tile = jnp.where(lane == at + 2 * i + 1, stat - high, tile)
    return tile


def put(ref, block, stats):
    width = block.shape[1]
    ref[:, :width] = block
    tail = tail_of(width)
    ref[:, tail] = with_stats(ref[:, tail].astype(F32), width, stats).astype(ref.dtype)


def put_halves(mine, theirs, block, stats):
    half = mine.shape[0]
    put(mine, block[:half], [stat[:half] for stat in stats])
    put(theirs, block[half:].astype(BF16), [stat[half:] for stat in stats])


def put_copies(ref, block, stats):
    put(ref.at[0], block, stats)
    whole = ref[0]
    for i in range(1, ref.shape[0]):
        ref[i] = whole


def summed(ref, columns):
    total = ref[0, :, columns].astype(F32)
    for i in range(1, ref.shape[0]):
        total = total + ref[i, :, columns].astype(F32)
    return total


def local(body, outs, *args, reuse=None):
    return pl.pallas_call(
        body,
        out_shape=tuple(jax.ShapeDtypeStruct(s, d) for s, d in outs),
        in_specs=[pl.BlockSpec(memory_space=pltpu.VMEM) for _ in args],
        out_specs=tuple(pl.BlockSpec(memory_space=pltpu.VMEM) for _ in outs),
        input_output_aliases=reuse or {},
        compiler_params=pltpu.CompilerParams(vmem_limit_bytes=16 << 20),
    )(*args)


def exchange(parts, axis):
    size = lax.axis_size(axis)
    if parts.ndim == 2:
        parts = parts.reshape(size, parts.shape[0] // size, parts.shape[1])
    return lax.all_to_all(parts, axis, 0, 0, tiled=True)


def flat(message):
    return message.reshape(message.shape[0] * message.shape[1], message.shape[2])


def rejoin(near, far, whole):
    half = near.shape[0]
    whole[:half] = near[...]
    whole[half:] = far[...]


def pair_step(width, count, mine, theirs, *rest):
    *held, out = rest
    for source, copy in zip(held[: len(held) // 2], held[len(held) // 2 :]):
        copy[...] = source[...]
    out[...] = (mine[...] + theirs[...].astype(F32)).astype(BF16)
    if count:
        tail = tail_of(width)
        tile = mine[:, tail] + theirs[:, tail].astype(F32)
        out[:, tail] = with_stats(tile, width, read_stats(tile, width, count)).astype(BF16)


def swap(values):
    return lax.ppermute(values, "core", [(0, 1), (1, 0)])


def gathered(copies):
    near = flat(exchange(copies, "rows"))
    return near, swap(near)


def reduced(mine, theirs, width, count, *held):
    *held, message = local(
        lambda *refs: pair_step(width, count, *refs),
        [*((x.shape, x.dtype) for x in held), (mine.shape, BF16)],
        mine,
        swap(theirs),
        *held,
    )
    return (exchange(message, "rows"), *held)


def gate_step(
    near, far, gains, gate_weight, up_weight, target_rows, ids, weights, out, inputs, *kept
):
    rejoin(near, far, inputs)
    for source, copy in zip((target_rows, ids, weights, gains), kept):
        copy[...] = source[...]
    width = gate_weight.shape[1]
    values = inputs[...].astype(F32)
    scaled = (values * gains[0:1]).astype(BF16)
    squares = jnp.sum(values * values, axis=1, keepdims=True)
    put(out, contract(scaled, gate_weight[...], 1, 0).astype(BF16), [squares])
    out[:, padded(width) : padded(width) + width] = contract(
        scaled, up_weight[...], 1, 0
    ).astype(BF16)


def active_step(model, width, message, gate, upward, gelu_gate, gelu_slope, out):
    (squares,) = read_stats(summed(message, tail_of(width)), width, 1)
    scale = lax.rsqrt(squares / model + EPS)
    gate_value = summed(message, slice(0, width)) * scale
    up_value = summed(message, slice(padded(width), padded(width) + width)) * scale
    value, slope = gelu_parts(gate_value)
    gate[...] = gate_value
    upward[...] = up_value
    gelu_gate[...] = value
    gelu_slope[...] = slope
    put_copies(out, (value * up_value).astype(BF16), [squares])


def branch_step(message, down_weight, target_rows, mine, theirs):
    hidden, width = down_weight.shape
    half = mine.shape[0]
    block = contract(message[:, :hidden], down_weight[...], 1, 0)
    mine[:, :width] = block[:half]
    theirs[:, :width] = block[half:].astype(BF16)
    mine[:, width : 2 * width] = target_rows[:half].astype(F32)
    theirs[:, width : 2 * width] = target_rows[half:]


def norm_step(message, inputs, gains, head, branch, target, out):
    del head
    width = branch.shape[1]
    both = summed(message, slice(0, 2 * width))
    value = both[:, :width]
    branch[...] = value
    target[...] = both[:, width:]
    bent = value * gains[1:2]
    own = inputs[...].astype(F32)
    stats = [
        jnp.sum(x, axis=1, keepdims=True) for x in (value * value, own * bent, bent * bent, own * own)
    ]
    lane = lax.broadcasted_iota(jnp.int32, out.shape[1:], 1)
    tile = jnp.zeros(out.shape[1:], F32)
    for i, stat in enumerate(stats):
        tile = jnp.where(lane == i, stat, tile)
    for i in range(out.shape[0]):
        out[i] = tile


def scale_step(model, message, branch, scales, out):
    tile = message[0]
    for i in range(1, message.shape[0]):
        tile = tile + message[i]
    lane = lax.broadcasted_iota(jnp.int32, tile.shape, 1)
    square, cross, bent, own = [
        jnp.sum(jnp.where(lane == i, tile, 0.0), axis=1, keepdims=True) for i in range(4)
    ]
    post = lax.rsqrt(square / model + EPS)
    final_squares = own + post * (2.0 * cross + post * bent)
    final = lax.rsqrt(jnp.maximum(final_squares, 0.0) / model + EPS)
    scales[...] = jnp.where(lane == 0, post, final)
    put_copies(out, branch[...].astype(BF16), [post, final])


def logit_step(part, piece, inputs, gains, head, *rest):
    out, final, message = rest[-3:]
    half, width = piece.shape[0], final.shape[1]
    rows = slice(part * half, (part + 1) * half)
    message[rows] = piece[...]
    post, scale = read_stats(piece[:, tail_of(width)].astype(F32), width, 2)
    resid = inputs[rows].astype(F32) + piece[:, :width].astype(F32) * post * gains[1:2]
    value = (resid * scale * gains[2:3]).astype(BF16)
    final[rows] = value
    for i in range(0, head.shape[1], CHUNK):
        columns = slice(i, i + CHUNK)
        out[rows, columns] = contract(value, head[:, columns], 1, 0).astype(BF16)


def soft_step(message, ids, out):
    rows, vocab = message.shape[1:]
    step = 256
    others = jnp.zeros((rows, step), F32)
    cross = jnp.zeros((rows, step), F32)
    target = jnp.zeros((rows, step), F32)
    lane = lax.broadcasted_iota(jnp.int32, (rows, step), 1)
    for i in range(vocab // step):
        columns = slice(i * step, (i + 1) * step)
        logits = summed(message, columns)
        hits = lane == ids[...] - i * step
        bent = jnp.tanh(logits / CAP)
        raised = jnp.where(hits, 0.0, jnp.exp(CAP * bent - CAP))
        sloped = raised * (1.0 - bent * bent)
        others = others + raised
        cross = cross + sloped * logits
        target = target + jnp.where(hits, logits, 0.0)
        part = sloped.astype(BF16)
        for j in range(out.shape[0]):
            out[j, :, columns] = part
    stats = [jnp.sum(x, axis=1, keepdims=True) for x in (others, cross, target)]
    tile = with_stats(jnp.zeros((rows, LANES), F32), vocab, stats).astype(BF16)
    for j in range(out.shape[0]):
        out[j, :, vocab : vocab + LANES] = tile


def row_step(start, message, head, out):
    vocab = head.shape[1]
    rows = slice(start, start + out.shape[0])
    stats = read_stats(message[rows, vocab : vocab + LANES].astype(F32), vocab, 3)
    put(out, contract(message[rows, :vocab], head[...], 1, 1).astype(out.dtype), stats)


def resid_step(
    model, message, target_rows, branch, inputs, scales, weights, gains, grad_resid, out
):
    width = branch.shape[1]
    others, cross, logit = read_stats(summed(message, tail_of(width)), width, 3)
    bent = jnp.tanh(logit / CAP)
    target = CAP * bent
    total = others + jnp.exp(target - CAP)
    logprob = target - CAP - jnp.log(total)
    spread = weights[...] / total
    pull = -spread * others * (1.0 - bent * bent)
    post = scales[:, 0:1]
    final = scales[:, 1:2]
    post_gain = gains[1:2]
    final_gain = gains[2:3]
    grad_final = spread * summed(message, slice(0, width)) + pull * target_rows[...]
    back_final = (spread * cross + pull * logit) / final
    value = branch[...]
    resid = inputs[...].astype(F32) + post * value * post_gain
    grad = final * grad_final * final_gain - resid * (
        final * final * final * back_final / model
    )
    grad_resid[...] = grad
    weighted = grad * post_gain
    back_post = jnp.sum(weighted * value, axis=1, keepdims=True)
    put_copies(
        out,
        (post * weighted).astype(BF16),
        [spread, pull, weights[...] * logprob, back_post],
    )


def down_step(copies_n, part, piece, branch, down_weight, *rest):
    out, message, loss = rest[-3:]
    hidden, width = down_weight.shape
    half = piece.shape[0]
    rows = slice(part * half, (part + 1) * half)
    tail = tail_of(width)
    message[rows] = piece[...]
    _, _, score, back_post = read_stats(piece[:, tail].astype(F32), width, 4)
    post, _ = read_stats(branch[rows, tail].astype(F32), width, 2)
    put(
        out.at[rows],
        contract(piece[:, :width], down_weight[...], 1, 1).astype(BF16),
        [back_post, post / copies_n],
    )
    out[rows, padded(hidden) : padded(hidden) + hidden] = contract(
        branch[rows, :width], down_weight[...], 1, 1
    ).astype(BF16)
    score = -jnp.sum(score, axis=0, keepdims=True) / out.shape[0]
    loss[...] = loss[...] + score if part else score


def hidden_step(model, message, gate, upward, gelu_gate, gelu_slope, out):
    width = gate.shape[1]
    start = padded(width)
    back_post, post = read_stats(summed(message, tail_of(width)), width, 2)
    grad = summed(message, slice(0, width)) - summed(message, slice(start, start + width)) * (
        post * post * post * back_post / model
    )
    gate_in = (grad * upward[...] * gelu_slope[...]).astype(BF16)
    up_in = (grad * gelu_gate[...]).astype(BF16)
    back = jnp.sum(
        gate_in.astype(F32) * gate[...] + up_in.astype(F32) * upward[...], axis=1, keepdims=True
    )
    put(out.at[0], gate_in, [back, back_post])
    out[0, :, start : start + width] = up_in
    whole = out[0]
    for i in range(1, out.shape[0]):
        out[i] = whole


def normed_step(
    model,
    message,
    gate_weight,
    up_weight,
    active,
    branch,
    weighted,
    gains,
    final,
    mine,
    theirs,
    rates,
    final_copy,
):
    final_copy[...] = final[...]
    width, hidden = gate_weight.shape
    start = padded(hidden)
    total = contract(message[:, :hidden], gate_weight[...], 1, 1) + contract(
        message[:, start : start + hidden], up_weight[...], 1, 1
    )
    back, back_post = read_stats(message[:, tail_of(hidden)].astype(F32), hidden, 2)
    (squares,) = read_stats(active[:, tail_of(hidden)].astype(F32), hidden, 1)
    scale = lax.rsqrt(squares / model + EPS)
    put_halves(mine, theirs, total * scale * gains[0:1], [scale * scale * back / model])
    (post,) = read_stats(branch[:, tail_of(width)].astype(F32), width, 1)
    spread, pull = read_stats(weighted[:, tail_of(width)].astype(F32), width, 2)
    lane = lax.broadcasted_iota(jnp.int32, rates.shape, 1)
    tile = jnp.where(lane == 0, spread, pull)
    tile = jnp.where(lane == 2, post * post * post * back_post / model, tile)
    rates[...] = jnp.where(lane == 3, scale, tile)


def last_step(message, grad_resid, inputs, out):
    width = out.shape[1]
    (back,) = read_stats(summed(message, tail_of(width)), width, 1)
    total = grad_resid[...] + summed(message, slice(0, width))
    out[...] = (total - inputs[...].astype(F32) * back).astype(BF16)


def shards(
    hidden,
    pre_gain,
    post_gain,
    final_gain,
    gate_weight,
    up_weight,
    down_weight,
    head_weight,
    token_ids,
    rewards,
):
    tok_dev, width = hidden.shape
    tokens = token_ids.shape[0]
    rows_n = lax.axis_size("rows")
    cols_n = lax.axis_size("width")
    model = width * cols_n
    ff = gate_weight.shape[1]
    vocab = head_weight.shape[1]
    sub = tokens // cols_n
    half = tokens // 2
    core = lax.axis_index("core")
    vocab_index = lax.axis_index("rows") * 2 + core
    width_index = lax.axis_index("width")
    gains = jnp.stack([pre_gain, post_gain, final_gain])

    weights = jnp.repeat(rewards, tokens // rewards.shape[0])
    own_weights = lax.dynamic_slice_in_dim(weights, vocab_index * tok_dev, tok_dev, 0)[:, None]
    ids = token_ids.reshape(rows_n, 2, tok_dev)
    ids = jnp.where(core == 0, jnp.swapaxes(ids, 0, 1), jnp.swapaxes(ids[:, ::-1], 0, 1))
    ids = ids.reshape(tokens) - vocab_index * vocab
    hits = jnp.arange(vocab, dtype=jnp.int32)[None, :] == ids[:, None]
    sub_ids = lax.dynamic_slice_in_dim(ids, width_index * sub, sub, 0)[:, None]
    target_part = contract(hits.astype(BF16), head_weight, 1, 1).astype(BF16)
    near, far = gathered(jnp.broadcast_to(hidden[None], (rows_n, tok_dev, width)))
    message, inputs, target_part, sub_ids, own_weights, gains = local(
        gate_step,
        [
            ((tokens, padded(ff) * 2), BF16),
            ((tokens, width), BF16),
            ((tokens, width), BF16),
            ((sub, 1), jnp.int32),
            ((tok_dev, 1), F32),
            ((3, width), F32),
        ],
        near,
        far,
        gains,
        gate_weight,
        up_weight,
        target_part,
        sub_ids,
        own_weights,
    )
    gate, upward, gelu_gate, gelu_slope, message = local(
        lambda *refs: active_step(model, ff, *refs),
        [((sub, ff), F32)] * 4 + [((cols_n, sub, padded(ff)), BF16)],
        exchange(message, "width"),
    )
    active = flat(exchange(message, "width"))
    mine, theirs = local(
        branch_step,
        [((half, width * 2), F32), ((half, width * 2), BF16)],
        active,
        down_weight,
        target_part,
    )
    branch, target_rows, message = local(
        norm_step,
        [((tok_dev, width), F32)] * 2 + [((cols_n, tok_dev, LANES), F32)],
        *reduced(mine, theirs, width * 2, 0),
        hidden,
        gains,
        head_weight,
    )
    scales, message = local(
        lambda *refs: scale_step(model, *refs),
        [((tok_dev, LANES), F32), ((rows_n, tok_dev, padded(width)), BF16)],
        exchange(message, "width"),
        branch,
    )
    near, far = gathered(message)
    filled = ()
    for part, piece in enumerate((near, far)):
        filled = local(
            lambda *refs, part=part: logit_step(part, *refs),
            [
                ((tokens, vocab), BF16),
                ((tokens, width), BF16),
                ((tokens, padded(width)), BF16),
            ],
            piece,
            inputs,
            gains,
            head_weight,
            *filled,
            reuse={4 + i: i for i in range(len(filled))},
        )
    message, final, branch_all = filled
    (message,) = local(
        soft_step,
        [((cols_n, sub, vocab + LANES), BF16)],
        exchange(message, "width"),
        sub_ids,
    )
    sloped = flat(exchange(message, "width"))
    halves = [((half, padded(width)), F32), ((half, padded(width)), BF16)]
    (theirs,) = local(lambda *refs: row_step(half, *refs), halves[1:], sloped, head_weight)
    (mine,) = local(lambda *refs: row_step(0, *refs), halves[:1], sloped, head_weight)
    grad_resid, message = local(
        lambda *refs: resid_step(model, *refs),
        [((tok_dev, width), F32), ((rows_n, tok_dev, padded(width)), BF16)],
        *reduced(mine, theirs, width, 3),
        target_rows,
        branch,
        hidden,
        scales,
        own_weights,
        gains,
    )
    near, far = gathered(message)
    filled = ()
    for part, piece in enumerate((near, far)):
        filled = local(
            lambda *refs, part=part: down_step(cols_n, part, *refs),
            [((tokens, padded(ff) * 2), BF16), ((tokens, padded(width)), BF16), ((1, 1), F32)],
            piece,
            branch_all,
            down_weight,
            *filled,
            reuse={3 + i: i for i in range(len(filled))},
        )
    message, weighted, loss = filled
    (message,) = local(
        lambda *refs: hidden_step(model, *refs),
        [((cols_n, sub, padded(ff) * 2), BF16)],
        exchange(message, "width"),
        gate,
        upward,
        gelu_gate,
        gelu_slope,
    )
    grads_in = flat(exchange(message, "width"))
    mine, theirs, rates, final = local(
        lambda *refs: normed_step(model, *refs),
        [*halves, ((tokens, LANES), F32), ((tokens, width), BF16)],
        grads_in,
        gate_weight,
        up_weight,
        active,
        branch_all,
        weighted,
        gains,
        final,
    )
    scale_pre = rates[:, 3:4]
    message, rates = reduced(mine, theirs, width, 1, rates)
    (grad_hidden,) = local(
        last_step,
        [((tok_dev, width), BF16)],
        message,
        grad_resid,
        hidden,
    )

    spread, pull, along, late_scale = [rates[:, i : i + 1] for i in range(4)]
    delta = (spread * sloped[:, :vocab].astype(F32) + jnp.where(hits, pull, 0.0)).astype(BF16)
    grad_head = contract(final, delta, 0, 0).astype(BF16)
    grad_branch = (
        weighted[:, :width].astype(F32) - branch_all[:, :width].astype(F32) * along
    ).astype(BF16)
    grad_down = contract(active[:, :ff], grad_branch, 0, 0).astype(BF16)
    normed = (inputs.astype(F32) * scale_pre * pre_gain).astype(BF16)
    grad_gate = contract(normed, grads_in[:, :ff], 0, 0).astype(BF16)
    normed = (inputs.astype(F32) * late_scale * pre_gain).astype(BF16)
    grad_up = contract(normed, grads_in[:, padded(ff) : padded(ff) + ff], 0, 0).astype(BF16)
    return (grad_hidden, grad_gate, grad_up, grad_down, grad_head, loss[0, 0])


def solution(mesh):
    devices = mesh.devices
    vocab = ("rows", "core")
    return jax.shard_map(
        shards,
        mesh=Mesh(
            devices.reshape(devices.shape[0] // 2, 2, devices.shape[1]), (*vocab, "width")
        ),
        in_specs=(
            P(vocab, "width"),
            P("width"),
            P("width"),
            P("width"),
            P("width", vocab),
            P("width", vocab),
            P(vocab, "width"),
            P("width", vocab),
            P(),
            P(),
        ),
        out_specs=(
            P(vocab, "width"),
            P("width", vocab),
            P("width", vocab),
            P(vocab, "width"),
            P("width", vocab),
            P(),
        ),
        check_vma=False,
    )
```

```python
import math

import jax
import jax.numpy as jnp
from jax import lax
from jax.experimental import pallas as pl
from jax.experimental.pallas import tpu as pltpu
from jax.sharding import Mesh
from jax.sharding import PartitionSpec as P

CAP = 30.0
EPS = 1e-06
ROOT_TWO_PI = math.sqrt(2.0 / math.pi)
BF16 = jnp.bfloat16
F32 = jnp.float32
LANES = 128
CHUNK = 512


def contract(left, right, left_dim, right_dim):
    return lax.dot_general(
        left, right, (((left_dim,), (right_dim,)), ((), ())), preferred_element_type=F32
    )


def gelu_parts(value):
    square = value * value
    bent = jnp.tanh(ROOT_TWO_PI * value * (1.0 + 0.044715 * square))
    half = 0.5 * (1.0 + bent)
    slope = half + 0.5 * value * (1.0 - bent * bent) * ROOT_TWO_PI * (1.0 + 3.0 * 0.044715 * square)
    return value * half, slope


def padded(width):
    return width // LANES * LANES + LANES


def pick(tile, at):
    lane = lax.broadcasted_iota(jnp.int32, tile.shape, 1)
    return jnp.sum(jnp.where((lane == at) | (lane == at + 1), tile, 0.0), axis=1, keepdims=True)


def read_stats(tile, width, count):
    return [pick(tile, width % LANES + 2 * i) for i in range(count)]


def tail_of(width):
    return slice(width // LANES * LANES, padded(width))


def with_stats(tile, width, stats):
    lane = lax.broadcasted_iota(jnp.int32, tile.shape, 1)
    at = width % LANES
    tile = jnp.where(lane < at, tile, 0.0)
    for i, stat in enumerate(stats):
        high = stat.astype(BF16).astype(F32)
        tile = jnp.where(lane == at + 2 * i, high, tile)
        tile = jnp.where(lane == at + 2 * i + 1, stat - high, tile)
    return tile


def put(ref, block, stats):
    width = block.shape[1]
    ref[:, :width] = block
    tail = tail_of(width)
    ref[:, tail] = with_stats(ref[:, tail].astype(F32), width, stats).astype(ref.dtype)


def put_halves(mine, theirs, block, stats):
    half = mine.shape[0]
    put(mine, block[:half], [stat[:half] for stat in stats])
    put(theirs, block[half:].astype(BF16), [stat[half:] for stat in stats])


def put_copies(ref, block, stats):
    put(ref.at[0], block, stats)
    whole = ref[0]
    for i in range(1, ref.shape[0]):
        ref[i] = whole


def summed(ref, columns):
    total = ref[0, :, columns].astype(F32)
    for i in range(1, ref.shape[0]):
        total = total + ref[i, :, columns].astype(F32)
    return total


def local(body, outs, *args, reuse=None, off_chip=(), scratch=()):
    return pl.pallas_call(
        body,
        out_shape=tuple(jax.ShapeDtypeStruct(s, d) for s, d in outs),
        in_specs=[
            pl.BlockSpec(memory_space=pltpu.HBM if i in off_chip else pltpu.VMEM)
            for i in range(len(args))
        ],
        scratch_shapes=scratch,
        out_specs=tuple(pl.BlockSpec(memory_space=pltpu.VMEM) for _ in outs),
        input_output_aliases=reuse or {},
        compiler_params=pltpu.CompilerParams(vmem_limit_bytes=16 << 20),
    )(*args)


def exchange(parts, axis):
    size = lax.axis_size(axis)
    if parts.ndim == 2:
        parts = parts.reshape(size, parts.shape[0] // size, parts.shape[1])
    return lax.all_to_all(parts, axis, 0, 0, tiled=True)


def flat(message):
    return message.reshape(message.shape[0] * message.shape[1], message.shape[2])


def rejoin(near, far, whole):
    half = near.shape[0]
    whole[:half] = near[...]
    whole[half:] = far[...]


def pair_step(width, count, mine, theirs, *rest):
    *held, out = rest
    for source, copy in zip(held[: len(held) // 2], held[len(held) // 2 :]):
        copy[...] = source[...]
    out[...] = (mine[...] + theirs[...].astype(F32)).astype(BF16)
    if count:
        tail = tail_of(width)
        tile = mine[:, tail] + theirs[:, tail].astype(F32)
        out[:, tail] = with_stats(tile, width, read_stats(tile, width, count)).astype(BF16)


def swap(values):
    return lax.ppermute(values, "core", [(0, 1), (1, 0)])


def gathered(copies):
    near = flat(exchange(copies, "rows"))
    return near, swap(near)


def reduced(mine, theirs, width, count, *held):
    *held, message = local(
        lambda *refs: pair_step(width, count, *refs),
        [*((x.shape, x.dtype) for x in held), (mine.shape, BF16)],
        mine,
        swap(theirs),
        *held,
    )
    return (exchange(message, "rows"), *held)


def gate_step(
    near, far, gains, gate_weight, up_weight, target_rows, ids, weights, out, inputs, *kept
):
    rejoin(near, far, inputs)
    for source, copy in zip((target_rows, ids, weights, gains), kept):
        copy[...] = source[...]
    width = gate_weight.shape[1]
    values = inputs[...].astype(F32)
    scaled = (values * gains[0:1]).astype(BF16)
    squares = jnp.sum(values * values, axis=1, keepdims=True)
    put(out, contract(scaled, gate_weight[...], 1, 0).astype(BF16), [squares])
    out[:, padded(width) : padded(width) + width] = contract(
        scaled, up_weight[...], 1, 0
    ).astype(BF16)


def active_step(model, width, message, gate, upward, gelu_gate, gelu_slope, out):
    (squares,) = read_stats(summed(message, tail_of(width)), width, 1)
    scale = lax.rsqrt(squares / model + EPS)
    gate_value = summed(message, slice(0, width)) * scale
    up_value = summed(message, slice(padded(width), padded(width) + width)) * scale
    value, slope = gelu_parts(gate_value)
    gate[...] = gate_value
    upward[...] = up_value
    gelu_gate[...] = value
    gelu_slope[...] = slope
    put_copies(out, (value * up_value).astype(BF16), [squares])


def branch_step(message, down_weight, target_rows, mine, theirs):
    hidden, width = down_weight.shape
    half = mine.shape[0]
    block = contract(message[:, :hidden], down_weight[...], 1, 0)
    mine[:, :width] = block[:half]
    theirs[:, :width] = block[half:].astype(BF16)
    mine[:, width : 2 * width] = target_rows[:half].astype(F32)
    theirs[:, width : 2 * width] = target_rows[half:]


def norm_step(message, inputs, gains, head, branch, target, out):
    del head
    width = branch.shape[1]
    both = summed(message, slice(0, 2 * width))
    value = both[:, :width]
    branch[...] = value
    target[...] = both[:, width:]
    bent = value * gains[1:2]
    own = inputs[...].astype(F32)
    stats = [
        jnp.sum(x, axis=1, keepdims=True) for x in (value * value, own * bent, bent * bent, own * own)
    ]
    lane = lax.broadcasted_iota(jnp.int32, out.shape[1:], 1)
    tile = jnp.zeros(out.shape[1:], F32)
    for i, stat in enumerate(stats):
        tile = jnp.where(lane == i, stat, tile)
    for i in range(out.shape[0]):
        out[i] = tile


def scale_step(model, message, branch, scales, out):
    tile = message[0]
    for i in range(1, message.shape[0]):
        tile = tile + message[i]
    lane = lax.broadcasted_iota(jnp.int32, tile.shape, 1)
    square, cross, bent, own = [
        jnp.sum(jnp.where(lane == i, tile, 0.0), axis=1, keepdims=True) for i in range(4)
    ]
    post = lax.rsqrt(square / model + EPS)
    final_squares = own + post * (2.0 * cross + post * bent)
    final = lax.rsqrt(jnp.maximum(final_squares, 0.0) / model + EPS)
    scales[...] = jnp.where(lane == 0, post, final)
    put_copies(out, branch[...].astype(BF16), [post, final])


def logit_step(part, piece, inputs, gains, head, *rest):
    out, final, message = rest[-3:]
    half, width = piece.shape[0], final.shape[1]
    rows = slice(part * half, (part + 1) * half)
    message[rows] = piece[...]
    post, scale = read_stats(piece[:, tail_of(width)].astype(F32), width, 2)
    resid = inputs[rows].astype(F32) + piece[:, :width].astype(F32) * post * gains[1:2]
    value = (resid * scale * gains[2:3]).astype(BF16)
    final[rows] = value
    for i in range(0, head.shape[1], CHUNK):
        columns = slice(i, i + CHUNK)
        out[rows, columns] = contract(value, head[:, columns], 1, 0).astype(BF16)


def soft_step(message, ids, out):
    rows, vocab = message.shape[1:]
    step = 256
    others = jnp.zeros((rows, step), F32)
    cross = jnp.zeros((rows, step), F32)
    target = jnp.zeros((rows, step), F32)
    lane = lax.broadcasted_iota(jnp.int32, (rows, step), 1)
    for i in range(vocab // step):
        columns = slice(i * step, (i + 1) * step)
        logits = summed(message, columns)
        hits = lane == ids[...] - i * step
        bent = jnp.tanh(logits / CAP)
        raised = jnp.where(hits, 0.0, jnp.exp(CAP * bent - CAP))
        sloped = raised * (1.0 - bent * bent)
        others = others + raised
        cross = cross + sloped * logits
        target = target + jnp.where(hits, logits, 0.0)
        part = sloped.astype(BF16)
        for j in range(out.shape[0]):
            out[j, :, columns] = part
    stats = [jnp.sum(x, axis=1, keepdims=True) for x in (others, cross, target)]
    tile = with_stats(jnp.zeros((rows, LANES), F32), vocab, stats).astype(BF16)
    for j in range(out.shape[0]):
        out[j, :, vocab : vocab + LANES] = tile


def row_step(message, head, mine, theirs):
    vocab = head.shape[1]
    total = contract(head[...], message[:, :vocab], 1, 1).T
    stats = read_stats(message[:, vocab : vocab + LANES].astype(F32), vocab, 3)
    put_halves(mine, theirs, total, stats)


def resid_step(
    model, message, target_rows, branch, inputs, scales, weights, gains, grad_resid, out
):
    width = branch.shape[1]
    others, cross, logit = read_stats(summed(message, tail_of(width)), width, 3)
    bent = jnp.tanh(logit / CAP)
    target = CAP * bent
    total = others + jnp.exp(target - CAP)
    logprob = target - CAP - jnp.log(total)
    spread = weights[...] / total
    pull = -spread * others * (1.0 - bent * bent)
    post = scales[:, 0:1]
    final = scales[:, 1:2]
    post_gain = gains[1:2]
    final_gain = gains[2:3]
    grad_final = spread * summed(message, slice(0, width)) + pull * target_rows[...]
    back_final = (spread * cross + pull * logit) / final
    value = branch[...]
    resid = inputs[...].astype(F32) + post * value * post_gain
    grad = final * grad_final * final_gain - resid * (
        final * final * final * back_final / model
    )
    grad_resid[...] = grad
    weighted = grad * post_gain
    back_post = jnp.sum(weighted * value, axis=1, keepdims=True)
    put_copies(
        out,
        (post * weighted).astype(BF16),
        [spread, pull, weights[...] * logprob, back_post],
    )


def down_step(copies_n, near, far, branch, down_weight, out, message, loss):
    rejoin(near, far, message)
    hidden, width = down_weight.shape
    tail = tail_of(width)
    _, _, score, back_post = read_stats(message[:, tail].astype(F32), width, 4)
    post, _ = read_stats(branch[:, tail].astype(F32), width, 2)
    put(
        out,
        contract(message[:, :width], down_weight[...], 1, 1).astype(BF16),
        [back_post, post / copies_n],
    )
    out[:, padded(hidden) : padded(hidden) + hidden] = contract(
        branch[:, :width], down_weight[...], 1, 1
    ).astype(BF16)
    loss[...] = -jnp.sum(score, axis=0, keepdims=True) / message.shape[0]


def hidden_step(model, message, gate, upward, gelu_gate, gelu_slope, out):
    width = gate.shape[1]
    start = padded(width)
    back_post, post = read_stats(summed(message, tail_of(width)), width, 2)
    grad = summed(message, slice(0, width)) - summed(message, slice(start, start + width)) * (
        post * post * post * back_post / model
    )
    gate_in = (grad * upward[...] * gelu_slope[...]).astype(BF16)
    up_in = (grad * gelu_gate[...]).astype(BF16)
    back = jnp.sum(
        gate_in.astype(F32) * gate[...] + up_in.astype(F32) * upward[...], axis=1, keepdims=True
    )
    put(out.at[0], gate_in, [back, back_post])
    out[0, :, start : start + width] = up_in
    whole = out[0]
    for i in range(1, out.shape[0]):
        out[i] = whole


def normed_step(
    model,
    message,
    gate_weight,
    up_weight,
    active,
    branch,
    weighted,
    gains,
    final,
    mine,
    theirs,
    rates,
    final_copy,
):
    final_copy[...] = final[...]
    width, hidden = gate_weight.shape
    start = padded(hidden)
    total = contract(message[:, :hidden], gate_weight[...], 1, 1) + contract(
        message[:, start : start + hidden], up_weight[...], 1, 1
    )
    back, back_post = read_stats(message[:, tail_of(hidden)].astype(F32), hidden, 2)
    (squares,) = read_stats(active[:, tail_of(hidden)].astype(F32), hidden, 1)
    scale = lax.rsqrt(squares / model + EPS)
    put_halves(mine, theirs, total * scale * gains[0:1], [scale * scale * back / model])
    (post,) = read_stats(branch[:, tail_of(width)].astype(F32), width, 1)
    spread, pull = read_stats(weighted[:, tail_of(width)].astype(F32), width, 2)
    lane = lax.broadcasted_iota(jnp.int32, rates.shape, 1)
    tile = jnp.where(lane == 0, spread, pull)
    tile = jnp.where(lane == 2, post * post * post * back_post / model, tile)
    rates[...] = jnp.where(lane == 3, scale, tile)


def last_step(message_far, grad_far, inputs_far, out, message, grad_resid, inputs, sems):
    pairs = ((message_far, message), (grad_far, grad_resid), (inputs_far, inputs))
    copies = [pltpu.make_async_copy(*pair, sems.at[i]) for i, pair in enumerate(pairs)]
    for copy in copies:
        copy.start()
    for copy in copies:
        copy.wait()
    width = out.shape[1]
    (back,) = read_stats(summed(message, tail_of(width)), width, 1)
    total = grad_resid[...] + summed(message, slice(0, width))
    out[...] = (total - inputs[...].astype(F32) * back).astype(BF16)


def shards(
    hidden,
    pre_gain,
    post_gain,
    final_gain,
    gate_weight,
    up_weight,
    down_weight,
    head_weight,
    token_ids,
    rewards,
):
    tok_dev, width = hidden.shape
    tokens = token_ids.shape[0]
    rows_n = lax.axis_size("rows")
    cols_n = lax.axis_size("width")
    model = width * cols_n
    ff = gate_weight.shape[1]
    vocab = head_weight.shape[1]
    sub = tokens // cols_n
    half = tokens // 2
    core = lax.axis_index("core")
    vocab_index = lax.axis_index("rows") * 2 + core
    width_index = lax.axis_index("width")
    gains = jnp.stack([pre_gain, post_gain, final_gain])

    weights = jnp.repeat(rewards, tokens // rewards.shape[0])
    own_weights = lax.dynamic_slice_in_dim(weights, vocab_index * tok_dev, tok_dev, 0)[:, None]
    ids = token_ids.reshape(rows_n, 2, tok_dev)
    ids = jnp.where(core == 0, jnp.swapaxes(ids, 0, 1), jnp.swapaxes(ids[:, ::-1], 0, 1))
    ids = ids.reshape(tokens) - vocab_index * vocab
    hits = jnp.arange(vocab, dtype=jnp.int32)[None, :] == ids[:, None]
    sub_ids = lax.dynamic_slice_in_dim(ids, width_index * sub, sub, 0)[:, None]
    target_part = contract(hits.astype(BF16), head_weight, 1, 1).astype(BF16)
    near, far = gathered(jnp.broadcast_to(hidden[None], (rows_n, tok_dev, width)))
    message, inputs, target_part, sub_ids, own_weights, gains = local(
        gate_step,
        [
            ((tokens, padded(ff) * 2), BF16),
            ((tokens, width), BF16),
            ((tokens, width), BF16),
            ((sub, 1), jnp.int32),
            ((tok_dev, 1), F32),
            ((3, width), F32),
        ],
        near,
        far,
        gains,
        gate_weight,
        up_weight,
        target_part,
        sub_ids,
        own_weights,
    )
    gate, upward, gelu_gate, gelu_slope, message = local(
        lambda *refs: active_step(model, ff, *refs),
        [((sub, ff), F32)] * 4 + [((cols_n, sub, padded(ff)), BF16)],
        exchange(message, "width"),
    )
    active = flat(exchange(message, "width"))
    mine, theirs = local(
        branch_step,
        [((half, width * 2), F32), ((half, width * 2), BF16)],
        active,
        down_weight,
        target_part,
    )
    branch, target_rows, message = local(
        norm_step,
        [((tok_dev, width), F32)] * 2 + [((cols_n, tok_dev, LANES), F32)],
        *reduced(mine, theirs, width * 2, 0),
        hidden,
        gains,
        head_weight,
    )
    scales, message = local(
        lambda *refs: scale_step(model, *refs),
        [((tok_dev, LANES), F32), ((rows_n, tok_dev, padded(width)), BF16)],
        exchange(message, "width"),
        branch,
    )
    near, far = gathered(message)
    filled = ()
    for part, piece in enumerate((near, far)):
        filled = local(
            lambda *refs, part=part: logit_step(part, *refs),
            [
                ((tokens, vocab), BF16),
                ((tokens, width), BF16),
                ((tokens, padded(width)), BF16),
            ],
            piece,
            inputs,
            gains,
            head_weight,
            *filled,
            reuse={4 + i: i for i in range(len(filled))},
        )
    message, final, branch_all = filled
    (message,) = local(
        soft_step,
        [((cols_n, sub, vocab + LANES), BF16)],
        exchange(message, "width"),
        sub_ids,
    )
    sloped = flat(exchange(message, "width"))
    halves = [((half, padded(width)), F32), ((half, padded(width)), BF16)]
    mine, theirs = local(row_step, halves, sloped, head_weight)
    grad_resid, message = local(
        lambda *refs: resid_step(model, *refs),
        [((tok_dev, width), F32), ((rows_n, tok_dev, padded(width)), BF16)],
        *reduced(mine, theirs, width, 3),
        target_rows,
        branch,
        hidden,
        scales,
        own_weights,
        gains,
    )
    near, far = gathered(message)
    message, weighted, loss = local(
        lambda *refs: down_step(cols_n, *refs),
        [((tokens, padded(ff) * 2), BF16), ((tokens, padded(width)), BF16), ((1, 1), F32)],
        near,
        far,
        branch_all,
        down_weight,
    )
    (message,) = local(
        lambda *refs: hidden_step(model, *refs),
        [((cols_n, sub, padded(ff) * 2), BF16)],
        exchange(message, "width"),
        gate,
        upward,
        gelu_gate,
        gelu_slope,
    )
    grads_in = flat(exchange(message, "width"))
    mine, theirs, rates, final = local(
        lambda *refs: normed_step(model, *refs),
        [*halves, ((tokens, LANES), F32), ((tokens, width), BF16)],
        grads_in,
        gate_weight,
        up_weight,
        active,
        branch_all,
        weighted,
        gains,
        final,
    )
    scale_pre = rates[:, 3:4]
    message, rates = reduced(mine, theirs, width, 1, rates)
    (grad_hidden,) = local(
        last_step,
        [((tok_dev, width), BF16)],
        message,
        pltpu.with_memory_space_constraint(grad_resid, pltpu.HBM),
        pltpu.with_memory_space_constraint(hidden, pltpu.HBM),
        off_chip=(0, 1, 2),
        scratch=(
            pltpu.VMEM((rows_n, tok_dev, padded(width)), BF16),
            pltpu.VMEM((tok_dev, width), F32),
            pltpu.VMEM((tok_dev, width), BF16),
            pltpu.SemaphoreType.DMA((3,)),
        ),
    )

    spread, pull, along, late_scale = [rates[:, i : i + 1] for i in range(4)]
    delta = (spread * sloped[:, :vocab].astype(F32) + jnp.where(hits, pull, 0.0)).astype(BF16)
    grad_head = contract(final, delta, 0, 0).astype(BF16)
    grad_branch = (
        weighted[:, :width].astype(F32) - branch_all[:, :width].astype(F32) * along
    ).astype(BF16)
    grad_down = contract(active[:, :ff], grad_branch, 0, 0).astype(BF16)
    normed = (inputs.astype(F32) * scale_pre * pre_gain).astype(BF16)
    grad_gate = contract(normed, grads_in[:, :ff], 0, 0).astype(BF16)
    normed = (inputs.astype(F32) * late_scale * pre_gain).astype(BF16)
    grad_up = contract(normed, grads_in[:, padded(ff) : padded(ff) + ff], 0, 0).astype(BF16)
    return (grad_hidden, grad_gate, grad_up, grad_down, grad_head, loss[0, 0])


def solution(mesh):
    devices = mesh.devices
    vocab = ("rows", "core")
    return jax.shard_map(
        shards,
        mesh=Mesh(
            devices.reshape(devices.shape[0] // 2, 2, devices.shape[1]), (*vocab, "width")
        ),
        in_specs=(
            P(vocab, "width"),
            P("width"),
            P("width"),
            P("width"),
            P("width", vocab),
            P("width", vocab),
            P(vocab, "width"),
            P("width", vocab),
            P(),
            P(),
        ),
        out_specs=(
            P(vocab, "width"),
            P("width", vocab),
            P("width", vocab),
            P(vocab, "width"),
            P("width", vocab),
            P(),
        ),
        check_vma=False,
    )
```
